32 devices in a mesh: dp: 16 (over z, x, core), mp: 2 (over y).
Axes of the slice: x: 2, y: 2, z: 4, core: 2. Of those that a mesh axis runs over, the one named last changes fastest.
Arguments:
- tokens: bfloat16 [12544, 768], P(('dp', 'mp')), may hold values from -6 to 6
- tissue: int32 [16, 784], P('dp'), may hold values from 0 to 1, as said below
- first_gain: float32 [768], replicated, may hold values from 0.5 to 1.5
- first_shift: float32 [768], replicated, may hold values from -3 to 3
- w_query: bfloat16 [768, 768], P(None, 'mp'), may hold values from -0.21875 to 0.21875
- b_query: float32 [768], P('mp'), may hold values from -3 to 3
- w_key: bfloat16 [768, 768], P(None, 'mp'), may hold values from -0.21875 to 0.21875
- w_value: bfloat16 [768, 768], P(None, 'mp'), may hold values from -0.21875 to 0.21875
- b_value: float32 [768], P('mp'), may hold values from -3 to 3
- w_output: bfloat16 [768, 768], P('mp'), may hold values from -1.75 to 1.75
- b_output: float32 [768], replicated, may hold values from -3 to 3
- second_gain: float32 [768], replicated, may hold values from 0.5 to 1.5
- second_shift: float32 [768], replicated, may hold values from -3 to 3
- w_upward: bfloat16 [768, 3072], P(None, 'mp'), may hold values from -0.21875 to 0.21875
- b_upward: float32 [3072], P('mp'), may hold values from -3 to 3
- w_down: bfloat16 [3072, 768], P('mp'), may hold values from -0.109375 to 0.109375
- b_down: float32 [768], replicated, may hold values from -3 to 3
- cotangent: bfloat16 [12544, 768], P(('dp', 'mp')), may hold values from -6 to 6
Outputs:
- output: bfloat16 [12544, 768], P(('dp', 'mp'))
- grad_tokens: float32 [12544, 768], P(('dp', 'mp'))
- grad_first_gain: float32 [768], replicated
- grad_first_shift: float32 [768], replicated
- grad_w_query: float32 [768, 768], P(None, 'mp')
- grad_b_query: float32 [768], P('mp')
- grad_w_key: float32 [768, 768], P(None, 'mp')
- grad_w_value: float32 [768, 768], P(None, 'mp')
- grad_b_value: float32 [768], P('mp')
- grad_w_output: float32 [768, 768], P('mp')
- grad_b_output: float32 [768], replicated
- grad_second_gain: float32 [768], replicated
- grad_second_shift: float32 [768], replicated
- grad_w_upward: float32 [768, 3072], P(None, 'mp')
- grad_b_upward: float32 [3072], P('mp')
- grad_w_down: float32 [3072, 768], P('mp')
- grad_b_down: float32 [768], replicated
The draws below stay inside these ranges and needn't reach their ends.
Inputs may be any that keep to these rules, and one draw needn't show every extreme that they name: `tissue`: every image has from 196 to 784 patches marked 1, in no particular places.
All inputs are finite; a program needn't handle non-finite values.
Results may differ from the reference program's by a relative error of at most 0.015.
Values may be sent and summed in bfloat16 or wider, within the bound.
No kernel may reach another device: no remote copies, remote signals or barrier semaphores. Data moves between devices by JAX's collectives and lax.ppermute only.
A program may use at most 128 MiB of HBM per device.

```python
import jax
import jax.numpy as jnp
from jax import lax

D = 768
HEADS = 12
HEAD = 64
FF = 3072
PATCHES = 784
IMG_GROUP = 1
IMAGES = 16
TOKENS = 12544
N_DP = 16


def draw_tissue(key, part):
    count_key, order_key = jax.random.split(jax.random.fold_in(key, 7))
    counts = jax.random.randint(count_key, (IMAGES, 1), PATCHES // 4, PATCHES + 1)
    ranking = jax.random.randint(order_key, (IMAGES, PATCHES), 0, 1 << 20) * PATCHES
    ranking = ranking + jnp.arange(PATCHES, dtype=jnp.int32)[None, :]
    places = jnp.argsort(jnp.argsort(ranking, axis=1, stable=True), axis=1, stable=True)
    return (places < counts).astype(jnp.int32)


def shard_levels(rng, extent, pieces, low, high):
    level, own = 1.0, jax.random.fold_in(rng, 6)
    for dim, blocks in pieces:
        heights = jnp.exp(jax.random.uniform(jax.random.fold_in(own, dim), (blocks,), jnp.float32, low / len(pieces), high / len(pieces)))
        level = level * jnp.repeat(heights, extent[dim] // blocks).reshape([-1 if axis == dim else 1 for axis in range(len(extent))])
    return level


def noise(own_key, extent, width, most, pieces=(), kind=jnp.bfloat16):
    entries = width * jax.random.normal(own_key, extent, jnp.float32)
    if pieces:
        entries = entries * shard_levels(own_key, extent, pieces, -0.22, 0.18)
    return jnp.clip(entries, -most, most).astype(kind)


def setup_inputs(seed: int = 0) -> dict:
    arg_keys = jax.random.split(jax.random.key(seed), 19)
    tokens = noise(arg_keys[0], (TOKENS, D), 1.0, 6.0, ((0, 32),))
    tissue = draw_tissue(jax.random.fold_in(arg_keys[18], 71), 0)
    first_gain = jnp.clip(1.0 + 0.1 * jax.random.normal(arg_keys[2], (D,), jnp.float32), 0.5, 1.5)
    first_shift = noise(arg_keys[3], (D,), 0.5, 3.0, (), jnp.float32)
    w_query = noise(arg_keys[4], (D, D), D ** -0.5, 0.21875, ((1, 2),))
    b_query = noise(arg_keys[5], (D,), 0.5, 3.0, ((0, 2),), jnp.float32)
    w_key = noise(arg_keys[6], (D, D), D ** -0.5, 0.21875, ((1, 2),))
    w_value = noise(arg_keys[7], (D, D), D ** -0.5, 0.21875, ((1, 2),))
    b_value = noise(arg_keys[8], (D,), 0.5, 3.0, ((0, 2),), jnp.float32)
    w_output = noise(arg_keys[9], (D, D), (D // 64) ** -0.5, 1.75, ((0, 2),))
    b_output = noise(arg_keys[10], (D,), 0.5, 3.0, (), jnp.float32)
    second_gain = jnp.clip(1.0 + 0.1 * jax.random.normal(arg_keys[11], (D,), jnp.float32), 0.5, 1.5)
    second_shift = noise(arg_keys[12], (D,), 0.5, 3.0, (), jnp.float32)
    w_upward = noise(arg_keys[13], (D, FF), D ** -0.5, 0.21875, ((1, 2),))
    b_upward = noise(arg_keys[14], (FF,), 0.5, 3.0, ((0, 2),), jnp.float32)
    w_down = noise(arg_keys[15], (FF, D), FF ** -0.5, 0.109375, ((0, 2),))
    b_down = noise(arg_keys[16], (D,), 0.5, 3.0, (), jnp.float32)
    cotangent = noise(arg_keys[17], (TOKENS, D), 1.0, 6.0, ((0, 32),))
    return {"tokens": tokens, "tissue": tissue, "first_gain": first_gain, "first_shift": first_shift, "w_query": w_query, "b_query": b_query, "w_key": w_key, "w_value": w_value, "b_value": b_value, "w_output": w_output, "b_output": b_output, "second_gain": second_gain, "second_shift": second_shift, "w_upward": w_upward, "b_upward": b_upward, "w_down": w_down, "b_down": b_down, "cotangent": cotangent}


epsilon = 1e-06
masked_score = -1e+30

@jax.custom_vjp
def low(v):
    return lax.optimization_barrier(v.astype(jnp.bfloat16)).astype(jnp.float32)

@jax.custom_vjp
def low_back(v):
    return v

def low_keep(v):
    return (low(v), None)

def low_pass(kept, grad):
    return (grad,)

def back_keep(v):
    return (v, None)

def back_low(kept, grad):
    return (low(grad),)
low.defvjp(low_keep, low_pass)
low_back.defvjp(back_keep, back_low)

def normalize(values, gain, shift):
    average = lax.optimization_barrier(jnp.mean(values, axis=-1, keepdims=True))
    centred = values - average
    spread = lax.optimization_barrier(jnp.mean(centred * centred, axis=-1, keepdims=True))
    return centred * lax.rsqrt(spread + epsilon) * gain + shift

def encoder_layer(block_rows, block_mask, params):
    first_gain, first_shift, w_query, b_query, w_key, w_value, b_value, w_output, b_output, second_gain, second_shift, w_upward, b_upward, w_down, b_down = params
    precise = lax.Precision.HIGHEST
    images = block_mask.shape[0]
    head_shape = (images, PATCHES, HEADS, HEAD)
    normed1 = low(normalize(block_rows, first_gain, first_shift))
    queries = low(low_back(jnp.dot(normed1, w_query, precision=precise) + b_query)).reshape(head_shape)
    key_rows = low(low_back(jnp.dot(normed1, w_key, precision=precise))).reshape(head_shape)
    value_rows = low(low_back(jnp.dot(normed1, w_value, precision=precise) + b_value)).reshape(head_shape)
    scores = low_back(jnp.einsum('ipha,iqha->ihpq', queries, key_rows, precision=precise) * HEAD ** (-0.5))
    scores = jnp.where(block_mask[:, None, None, :] > 0, scores, masked_score)
    highest = lax.optimization_barrier(jnp.max(scores, axis=-1, keepdims=True))
    log_total = highest + jnp.log(lax.optimization_barrier(jnp.sum(jnp.exp(scores - highest), axis=-1, keepdims=True)))
    chance_low = low(jnp.exp(scores - log_total))
    context = jnp.einsum('ihpq,iqha->ipha', chance_low, value_rows, precision=precise)
    context = low_back(low(context.reshape(images * PATCHES, HEADS * HEAD)))
    attention = low_back(jnp.dot(context, w_output, precision=precise) + b_output)
    hidden1 = block_rows + attention
    normed2 = low(normalize(hidden1, second_gain, second_shift))
    pre_gelu = low_back(jnp.dot(normed2, w_upward, precision=precise) + b_upward)
    activated = low(jax.nn.gelu(pre_gelu, approximate=False))
    return hidden1 + jnp.dot(activated, w_down, precision=precise) + b_down

def reference(tokens, tissue, first_gain, first_shift, w_query, b_query, w_key, w_value, b_value, w_output, b_output, second_gain, second_shift, w_upward, b_upward, w_down, b_down, cotangent):
    params = tuple((entry.astype(jnp.float32) for entry in (first_gain, first_shift, w_query, b_query, w_key, w_value, b_value, w_output, b_output, second_gain, second_shift, w_upward, b_upward, w_down, b_down)))
    group_rows = IMG_GROUP * PATCHES
    inputs = tokens.astype(jnp.float32).reshape(N_DP, group_rows, D)
    grads_in = cotangent.astype(jnp.float32).reshape(N_DP, group_rows, D)
    masks = tissue.reshape(N_DP, IMG_GROUP, PATCHES)

    def advance(totals, block_data):
        block_rows, block_mask, block_grad = block_data

        def apply_layer(rows_in, params_in):
            return encoder_layer(rows_in, block_mask, params_in)
        result, backward = jax.vjp(apply_layer, block_rows, params)
        grad_rows, grad_params = backward(block_grad)
        totals = tuple((total + piece for total, piece in zip(totals, grad_params)))
        return (totals, (result.astype(jnp.bfloat16), grad_rows))
    initial = tuple((jnp.zeros_like(entry) for entry in params))
    totals, (results, grad_rows) = lax.scan(advance, initial, (inputs, masks, grads_in))
    return (results.reshape(TOKENS, D), grad_rows.reshape(TOKENS, D), totals[0], totals[1], totals[2], totals[3], totals[4], totals[5], totals[6], totals[7], totals[8], totals[9], totals[10], totals[11], totals[12], totals[13], totals[14])
```

```python
import functools

import jax
import jax.numpy as jnp
from jax import lax
from jax.experimental import pallas as pl
from jax.experimental.pallas import tpu as pltpu
from jax.sharding import PartitionSpec as P

HEAD = 64
LANES = 256
epsilon = 1e-06
masked_score = -1e30
low, wide = jnp.bfloat16, jnp.float32
params = pltpu.CompilerParams(vmem_limit_bytes=48 << 20)


def cost(flops, moved, exps=0):
    return pl.CostEstimate(flops=flops, bytes_accessed=moved, transcendentals=exps)


def whole(array):
    return pl.BlockSpec(array.shape, lambda *_: (0,) * len(array.shape))


def shaped(shape, kind):
    return jax.ShapeDtypeStruct(shape, kind)


def mm(left, right, left_dim, right_dim):
    return lax.dot_general(
        left, right, (((left_dim,), (right_dim,)), ((), ())), preferred_element_type=wide
    )


def normalize(values, gain, shift):
    centred = values - jnp.mean(values, axis=-1, keepdims=True)
    spread = jnp.mean(centred * centred, axis=-1, keepdims=True)
    return centred * lax.rsqrt(spread + epsilon) * gain + shift


def normalize_back(values, gain, grad):
    centred = values - jnp.mean(values, axis=-1, keepdims=True)
    inverse = lax.rsqrt(jnp.mean(centred * centred, axis=-1, keepdims=True) + epsilon)
    unit = centred * inverse
    scaled = grad * gain
    by_values = inverse * (
        scaled
        - jnp.mean(scaled, axis=-1, keepdims=True)
        - unit * jnp.mean(scaled * unit, axis=-1, keepdims=True)
    )
    return by_values, jnp.sum(grad * unit, axis=0), jnp.sum(grad, axis=0)


def spans(extent):
    edges = list(range(0, extent, LANES))
    if len(edges) > 1 and extent - edges[-1] < LANES // 2:
        edges.pop()
    return list(zip(edges, edges[1:] + [extent]))


def split_three(row):
    first = row.astype(low).astype(wide)
    second = (row - first).astype(low).astype(wide)
    return first, second, row - first - second


def head_rows(part, width, head):
    return pl.ds(pl.multiple_of(part * width + head * HEAD, HEAD), HEAD)


def attention_forward_kernel(
    own_ref, other_ref, vectors_ref, w_ref, b_ref, bias_ref, qkv_ref, own_context_ref, other_context_ref, exact_ref,
    log_ref, turned_ref
):
    head = pl.program_id(0)
    own = own_ref.shape[0]
    rows = 2 * own
    width = w_ref.shape[0] // 3

    @pl.when(head == 0)
    def _():
        gain, shift = vectors_ref[0:1], vectors_ref[1:2]
        normed = jnp.concatenate(
            [normalize(ref[...].astype(wide), gain, shift) for ref in (own_ref, other_ref)], axis=0
        ).astype(low)
        turned_ref[...] = normed.T
        for part in range(3):
            at = slice(part * width, (part + 1) * width)
            qkv_ref[at] = (mm(w_ref[at], normed, 1, 1) + b_ref[at]).astype(low)

    queries = qkv_ref[head_rows(0, width, head)] * jnp.array(HEAD**-0.5, low)
    keys = jnp.concatenate([qkv_ref[head_rows(1, width, head)], bias_ref[...]], axis=0).T
    values = qkv_ref[head_rows(2, width, head)]
    index = lax.broadcasted_iota(jnp.int32, (16, rows), 0)
    queries = jnp.concatenate([queries, jnp.where(index == 0, 1.0, 0.0).astype(low)], axis=0)
    pieces = []
    for start, stop in spans(rows):
        scores = mm(keys, queries[:, start:stop], 1, 0)
        highest = jnp.max(scores, axis=0, keepdims=True)
        powers = jnp.exp(scores - highest)
        total = jnp.sum(powers, axis=0, keepdims=True)
        log_ref[0, :, start:stop] = highest + jnp.log(total)
        pieces.append(mm(values, powers.astype(low), 1, 0) * (1.0 / total))
    context = jnp.concatenate(pieces, axis=1)
    exact_ref[...] = context
    context = context.astype(low)
    own_context_ref[...] = context[:, :own]
    other_context_ref[...] = context[:, own:]


def attention_forward(own, other, vectors, w, b, bias):
    count, features = own.shape
    width = w.shape[0] // 3
    rows = 2 * count
    by_head = lambda columns: pl.BlockSpec((HEAD, columns), lambda head: (head, 0))
    return pl.pallas_call(
        attention_forward_kernel,
        name="attention_forward",
        grid=(width // HEAD,),
        in_specs=[whole(a) for a in (own, other, vectors, w, b, bias)],
        out_specs=[
            pl.BlockSpec((3 * width, rows), lambda head: (0, 0)),
            by_head(count),
            by_head(count),
            by_head(rows),
            pl.BlockSpec((1, 1, rows), lambda head: (head, 0, 0)),
            pl.BlockSpec((features, rows), lambda head: (0, 0)),
        ],
        out_shape=[
            shaped((3 * width, rows), low),
            shaped((width, count), low),
            shaped((width, count), low),
            shaped((width, rows), wide),
            shaped((width // HEAD, 1, rows), wide),
            shaped((features, rows), low),
        ],
        compiler_params=params,
        cost_estimate=cost(10 * 10**9, 10**7, 4 * 10**6),
    )(own, other, vectors, w, b, bias)


def attention_backward_kernel(qkv_ref, exact_ref, log_ref, bias_ref, own_grad_ref, other_grad_ref, out_ref):
    head = pl.program_id(0)
    rows = qkv_ref.shape[1]
    width = qkv_ref.shape[0] // 3
    scale = HEAD**-0.5
    queries = qkv_ref[head_rows(0, width, head)] * jnp.array(scale, low)
    keys = qkv_ref[head_rows(1, width, head)]
    values = qkv_ref[head_rows(2, width, head)]
    grads = jnp.concatenate([own_grad_ref[...], other_grad_ref[...]], axis=1)
    overlap = jnp.sum(grads.astype(wide) * exact_ref[...], axis=0, keepdims=True)
    index = lax.broadcasted_iota(jnp.int32, (16, rows), 0)

    def stack(top, *extra):
        block = jnp.zeros((16, rows), wide)
        for place, row in enumerate(extra):
            block = jnp.where(index == place, row, block)
        return jnp.concatenate([top, block.astype(low)], axis=0)

    bias = bias_ref[0:1].astype(wide)
    queries_more = stack(queries, 1.0, *split_three(-log_ref[0]))
    keys_more = stack(keys, bias, 1.0, 1.0, 1.0).T
    grads_more = stack(grads, *split_three(-overlap))
    values_more = stack(values, 1.0, 1.0, 1.0).T
    grad_keys = jnp.zeros((HEAD, rows), wide)
    grad_values = jnp.zeros((HEAD, rows), wide)
    for start, stop in spans(rows):
        at = slice(start, stop)
        chances = jnp.exp(mm(keys_more, queries_more[:, at], 1, 0))
        grad_values = grad_values + mm(grads[:, at], chances.astype(low), 1, 1)
        grad_scores = (chances * mm(values_more, grads_more[:, at], 1, 0)).astype(low)
        out_ref[head_rows(0, width, head), at] = (mm(keys, grad_scores, 1, 0) * scale).astype(low)
        grad_keys = grad_keys + mm(queries[:, at], grad_scores, 1, 1)
    out_ref[head_rows(1, width, head)] = grad_keys.astype(low)
    out_ref[head_rows(2, width, head)] = grad_values.astype(low)


def attention_backward(qkv, exact, logs, bias, own_grad, other_grad):
    rows = qkv.shape[1]
    width = qkv.shape[0] // 3
    by_head = lambda columns: pl.BlockSpec((HEAD, columns), lambda head: (head, 0))
    return pl.pallas_call(
        attention_backward_kernel,
        name="attention_backward",
        grid=(width // HEAD,),
        in_specs=[
            whole(qkv),
            by_head(rows),
            pl.BlockSpec((1, 1, rows), lambda head: (head, 0, 0)),
            whole(bias),
            by_head(rows // 2),
            by_head(rows // 2),
        ],
        out_specs=whole(qkv),
        out_shape=shaped(qkv.shape, low),
        compiler_params=params,
        cost_estimate=cost(10 * 10**9, 10**7, 4 * 10**6),
    )(qkv, exact, logs, bias, own_grad, other_grad)


def gelu_both(values):
    below = 0.5 * (1.0 + lax.erf(values * (0.5**0.5)))
    density = jnp.exp(values * values * -0.5) * (2.0 * jnp.pi) ** -0.5
    return values * below, below + values * density


def feed_forward_kernel(
    tokens_ref, mine_ref, peer_ref, w_mine_ref, w_peer_ref, vectors_ref, cotangent_ref, up_ref, b_up_ref, down_ref,
    hidden_ref, normed_ref, activated_ref, grad_pre_ref, grad_normed_ref, branch_ref, grad_b_ref, grad_sum, sum_
):
    step = pl.program_id(0)

    @pl.when(step == 0)
    def _():
        attention = mm(mine_ref[...], w_mine_ref[...], 0, 0) + mm(peer_ref[...], w_peer_ref[...], 0, 0)
        hidden = tokens_ref[...].astype(wide) + (attention + vectors_ref[2:3])
        hidden_ref[...] = hidden
        normed_ref[...] = normalize(hidden, vectors_ref[3:4], vectors_ref[4:5]).astype(low)
        grad_sum[...] = jnp.zeros_like(grad_sum)
        sum_[...] = jnp.zeros_like(sum_)

    up, down = up_ref[...], down_ref[...]
    pre_gelu = mm(normed_ref[...], up, 1, 0) + b_up_ref[...]
    grad_active = mm(cotangent_ref[...], down, 1, 1)
    activated, slope = gelu_both(pre_gelu)
    activated = activated.astype(low)
    grad_pre = (grad_active * slope).astype(low)
    activated_ref[...] = activated
    grad_pre_ref[...] = grad_pre
    grad_b_ref[...] = jnp.sum(grad_pre.astype(wide), axis=0, keepdims=True)
    grad_sum[...] += mm(grad_pre, up, 1, 1)
    sum_[...] += mm(activated, down, 1, 0)

    @pl.when(step == pl.num_programs(0) - 1)
    def _():
        grad_normed_ref[...] = grad_sum[...].astype(low)
        branch_ref[...] = sum_[...].astype(low)


def feed_forward(tokens, mine, peer, w_mine, w_peer, vectors, cotangent, up, b_up, down):
    rows, features = tokens.shape
    units = up.shape[1]
    block = 512
    hidden_units = pl.BlockSpec((rows, block), lambda step: (0, step))
    return pl.pallas_call(
        feed_forward_kernel,
        name="feed_forward",
        grid=(units // block,),
        in_specs=[whole(a) for a in (tokens, mine, peer, w_mine, w_peer, vectors, cotangent)]
        + [
            pl.BlockSpec((features, block), lambda step: (0, step)),
            pl.BlockSpec((1, block), lambda step: (0, step)),
            pl.BlockSpec((block, features), lambda step: (step, 0)),
        ],
        out_specs=[whole(tokens), whole(tokens), hidden_units, hidden_units, whole(tokens), whole(tokens)]
        + [pl.BlockSpec((1, block), lambda step: (0, step))],
        out_shape=[
            shaped((rows, features), wide),
            shaped((rows, features), low),
            shaped((rows, units), low),
            shaped((rows, units), low),
            shaped((rows, features), low),
            shaped((rows, features), low),
            shaped((1, units), wide),
        ],
        scratch_shapes=[pltpu.VMEM((rows, features), wide), pltpu.VMEM((rows, features), wide)],
        compiler_params=params,
        cost_estimate=cost(5 * 10**9, 10**7, 10**6),
    )(tokens, mine, peer, w_mine, w_peer, vectors, cotangent, up, b_up, down)


def middle_kernel(
    part_ref, came_ref, hidden_ref, cotangent_ref, vectors_ref, w_mine_ref, w_peer_ref,
    grad_hidden_ref, branch_ref, mine_ref, peer_ref, sums_ref
):
    grad = part_ref[...].astype(wide) + came_ref[...].astype(wide)
    cotangent = cotangent_ref[...].astype(wide)
    by_hidden, by_gain, by_shift = normalize_back(hidden_ref[...], vectors_ref[3:4], grad)
    grad_hidden = by_hidden + cotangent
    grad_hidden_ref[...] = grad_hidden
    branch = grad_hidden.astype(low)
    branch_ref[...] = branch
    mine_ref[...] = mm(w_mine_ref[...], branch, 1, 1).astype(low)
    peer_ref[...] = mm(w_peer_ref[...], branch, 1, 1).astype(low)
    sums_ref[...] = jnp.zeros_like(sums_ref)
    sums_ref[0:1] = jnp.sum(branch.astype(wide), axis=0, keepdims=True)
    sums_ref[1:2] = by_gain[None]
    sums_ref[2:3] = by_shift[None]
    sums_ref[3:4] = jnp.sum(cotangent, axis=0, keepdims=True)


def middle(part, came, hidden, cotangent, vectors, w_mine, w_peer):
    rows, features = part.shape
    width = w_mine.shape[0]
    args = (part, came, hidden, cotangent, vectors, w_mine, w_peer)
    return pl.pallas_call(
        middle_kernel,
        name="second_norm_backward",
        out_shape=[
            shaped((rows, features), wide),
            shaped((rows, features), low),
            shaped((width, rows), low),
            shaped((width, rows), low),
            shaped((8, features), wide),
        ],
        compiler_params=params,
        cost_estimate=cost(10**9, 5 * 10**6),
    )(*args)


def last_kernel(part_ref, came_ref, tokens_ref, grad_hidden_ref, vectors_ref, out_ref, sums_ref):
    grad = part_ref[...].astype(wide) + came_ref[...].astype(wide)
    by_tokens, by_gain, by_shift = normalize_back(tokens_ref[...].astype(wide), vectors_ref[0:1], grad)
    out_ref[...] = grad_hidden_ref[...] + by_tokens
    sums_ref[...] = jnp.zeros_like(sums_ref)
    sums_ref[0:1] = by_gain[None]
    sums_ref[1:2] = by_shift[None]


def last(part, came, tokens, grad_hidden, vectors):
    rows, features = part.shape
    return pl.pallas_call(
        last_kernel,
        name="first_norm_backward",
        out_shape=[shaped((rows, features), wide), shaped((8, features), wide)],
        compiler_params=params,
        cost_estimate=cost(10**8, 5 * 10**6),
    )(part, came, tokens, grad_hidden, vectors)


def by_inputs_kernel(grads_ref, w_ref, own_ref, other_ref, sums_ref):
    own = own_ref.shape[0]
    grads = grads_ref[...]
    other_ref[...] = mm(grads[:, own:], w_ref[...], 0, 0).astype(low)
    own_ref[...] = mm(grads[:, :own], w_ref[...], 0, 0).astype(low)
    sums_ref[...] = mm(jnp.ones((8, grads.shape[1]), low), grads, 1, 1)


def by_inputs(grads, w):
    rows, features = grads.shape[1] // 2, w.shape[1]
    return pl.pallas_call(
        by_inputs_kernel,
        name="first_normed_gradient",
        out_shape=[
            shaped((rows, features), low),
            shaped((rows, features), low),
            shaped((8, grads.shape[0]), wide),
        ],
        compiler_params=params,
        cost_estimate=cost(2 * 10**9, 5 * 10**6),
    )(grads, w)


def weight_gradient_kernel(core_ref, *refs, dims, pairs):
    away_ref, kept_ref = refs[2 * pairs :]
    step, blocks = pl.program_id(0), pl.num_programs(0) // 2
    total = mm(refs[0][...], refs[1][...], *dims)
    for j in range(1, pairs):
        total = total + mm(refs[2 * j][...], refs[2 * j + 1][...], *dims)

    @pl.when(step < blocks)
    def _():
        away_ref[...] = total.astype(low)

    @pl.when(step >= blocks)
    def _():
        kept_ref[...] = total


def weight_gradient(core, pairs, dims, block):
    left, right = pairs[0]
    rows, columns = left.shape[1 - dims[0]], right.shape[1 - dims[1]]
    half = rows // 2
    blocks = half // block

    def place(step, core_ref):
        side = jnp.where(step < blocks, 1 - core_ref[0], core_ref[0])
        at = side * blocks + lax.rem(step, blocks)
        return (0, at) if dims[0] == 0 else (at, 0)

    specs, flat = [], []
    for left, right in pairs:
        shape = (left.shape[0], block) if dims[0] == 0 else (block, left.shape[1])
        specs += [pl.BlockSpec(shape, place), whole(right)]
        flat += [left, right]
    return pl.pallas_call(
        functools.partial(weight_gradient_kernel, dims=dims, pairs=len(pairs)),
        name="weight_gradient",
        grid_spec=pltpu.PrefetchScalarGridSpec(
            num_scalar_prefetch=1,
            grid=(2 * blocks,),
            in_specs=specs,
            out_specs=[
                pl.BlockSpec((block, columns), lambda step, _: (jnp.minimum(step, blocks - 1), 0)),
                pl.BlockSpec((block, columns), lambda step, _: (jnp.maximum(step - blocks, 0), 0)),
            ],
        ),
        out_shape=[shaped((half, columns), low), shaped((half, columns), wide)],
        compiler_params=params,
        cost_estimate=cost(2 * 10**9, 10**7),
    )(core, *flat)


def after(value, *others):
    return lax.optimization_barrier((value, *others))[0]


def swap_mp(value):
    return lax.ppermute(value, "mp", [(0, 1), (1, 0)])


def swap_dp(value, mask, count):
    return lax.ppermute(value, "dp", [(i, i ^ mask) for i in range(count)])


def rows_at(value, at, rows):
    return lax.dynamic_slice_in_dim(value, at * rows, rows, 0)


def rows_set(value, block, at):
    return lax.dynamic_update_slice_in_dim(value, block, at * block.shape[0], 0)


def chip_sum(block, radices, stride, chip, count):
    if not radices:
        return block.astype(low)
    radix = radices[0]
    digit = (chip // stride) & (radix - 1)
    rows = block.shape[0] // radix
    total = rows_at(block, digit, rows)
    came = [
        swap_dp(rows_at(block, digit ^ j, rows).astype(low), 2 * stride * j, count) for j in range(1, radix)
    ]
    for piece in came:
        total = total + piece.astype(wide)
    mine = chip_sum(total, radices[1:], stride * radix, chip, count)
    gathered = rows_set(jnp.zeros(block.shape, low), mine, digit)
    for j in range(1, radix):
        gathered = rows_set(gathered, swap_dp(mine, 2 * stride * j, count), digit ^ j)
    return gathered


def device_sum(away, kept, radices, place, count):
    core, chip = place & 1, place >> 1
    half = kept + swap_dp(away, 1, count).astype(wide)
    half = chip_sum(half, radices, 1, chip, count)
    other = swap_dp(half, 1, count)
    first = jnp.where(core == 0, half, other)
    second = jnp.where(core == 0, other, half)
    return jnp.concatenate([first, second], axis=0).astype(wide)


def small_sum(block, count):
    mask = 1
    while mask < count:
        block = block + swap_dp(block, mask, count)
        mask *= 2
    return block


def local(
    count,
    tokens,
    tissue,
    first_gain,
    first_shift,
    w_query,
    b_query,
    w_key,
    w_value,
    b_value,
    w_output,
    b_output,
    second_gain,
    second_shift,
    w_upward,
    b_upward,
    w_down,
    b_down,
    cotangent,
):
    place, side = lax.axis_index("dp"), lax.axis_index("mp")
    core = place & 1
    core_list = core.reshape(1)
    own = tokens.shape[0]
    width = w_query.shape[1]
    bits = (count // 2).bit_length() - 1
    binary = (2,) * bits

    tokens_other = swap_mp(tokens)
    w_peer = swap_mp(after(w_output, tokens_other))
    cotangent_other = swap_mp(after(cotangent, tokens_other))
    valid = tissue[0] > 0
    valid = jnp.where(side == 0, valid, jnp.roll(valid, own))
    bias = jnp.where(valid, 0.0, masked_score).astype(low)
    bias = jnp.pad(bias[None], ((0, 15), (0, 0)))
    vectors = jnp.stack([first_gain, first_shift, b_output, second_gain, second_shift, b_down])
    vectors = jnp.pad(vectors, ((0, 2), (0, 0)))
    w_stack = jnp.concatenate([w_query, w_key, w_value], axis=1).T
    b_stack = jnp.concatenate([b_query, jnp.zeros_like(b_query), b_value])[:, None]

    qkv, own_context, other_context, exact, logs, turned = attention_forward(
        tokens, tokens_other, vectors, w_stack, b_stack, bias
    )
    peer_own = swap_mp(other_context)
    peer_other = swap_mp(own_context)
    b_up = b_upward[None]
    shared = (w_upward, b_up, w_down)
    _, normed_b, active_b, pre_b, part_b, branch_b, sum_b = feed_forward(
        tokens_other, other_context, peer_other, w_output, w_peer, vectors, cotangent_other, *shared
    )
    came = swap_mp(part_b)
    hidden, normed_a, active_a, pre_a, part_a, branch_a, sum_a = feed_forward(
        tokens, own_context, peer_own, w_output, w_peer, vectors, cotangent, *shared
    )
    pieces_down = weight_gradient(
        core_list, ((active_a, cotangent), (active_b, cotangent_other)), (0, 0), w_down.shape[0] // 2
    )
    grad_down = device_sum(*pieces_down, binary, place, count)
    pieces_up = weight_gradient(
        core_list, ((normed_a, pre_a), (normed_b, pre_b)), (0, 0), w_upward.shape[0] // 2
    )
    grad_upward = device_sum(*pieces_up, binary, place, count)

    grad_hidden, grad_branch, mine_own, peer_grad, sums = middle(
        part_a, came, hidden, cotangent, vectors, w_output, w_peer
    )
    mine_other = swap_mp(peer_grad)
    branch_other = swap_mp(after(grad_branch, mine_other))
    branch_came = swap_mp(after(branch_b, mine_other))
    output = (
        hidden + (branch_a.astype(wide) + branch_came.astype(wide) + b_down)
    ).astype(low)
    grads = attention_backward(qkv, exact, logs, bias, mine_own, mine_other)
    pieces_out = weight_gradient(
        core_list, ((own_context, grad_branch), (other_context, branch_other)), (1, 0), width // 2
    )
    grad_woutput = device_sum(*pieces_out, binary, place, count)
    pieces_stack = weight_gradient(core_list, ((turned, grads),), (1, 1), turned.shape[0] // 2)
    tail = (2, 4) + (2,) * (bits - 3) if bits >= 3 else binary
    grad_stack = device_sum(*pieces_stack, tail, place, count)
    part_a, part_b, stack_sums = by_inputs(grads, w_stack)
    came = swap_mp(part_b)
    grad_tokens, sums_first = last(part_a, came, tokens, grad_hidden, vectors)

    sums = jnp.concatenate([sums_first[:2], sums[:4]], axis=0)
    sums = sums + swap_mp(sums)
    columns = sums.shape[1]
    split = jnp.concatenate(
        [stack_sums[0, :width], stack_sums[0, 2 * width :], (sum_a + sum_b)[0]]
    ).reshape(-1, columns)
    small = small_sum(jnp.concatenate([sums, split], axis=0), count)
    split = small[6:].reshape(-1)
    return (
        output,
        grad_tokens,
        small[0],
        small[1],
        grad_stack[:, :width],
        split[:width],
        grad_stack[:, width : 2 * width],
        grad_stack[:, 2 * width :],
        split[width : 2 * width],
        grad_woutput,
        small[2],
        small[3],
        small[4],
        grad_upward,
        split[2 * width :],
        grad_down,
        small[5],
    )


def solution(mesh):
    in_specs = (
        P(("dp", "mp"), None),
        P("dp", None),
        P(),
        P(),
        P(None, "mp"),
        P("mp"),
        P(None, "mp"),
        P(None, "mp"),
        P("mp"),
        P("mp", None),
        P(),
        P(),
        P(),
        P(None, "mp"),
        P("mp"),
        P("mp", None),
        P(),
        P(("dp", "mp"), None),
    )
    out_specs = (
        P(("dp", "mp"), None),
        P(("dp", "mp"), None),
        P(),
        P(),
        P(None, "mp"),
        P("mp"),
        P(None, "mp"),
        P(None, "mp"),
        P("mp"),
        P("mp", None),
        P(),
        P(),
        P(),
        P(None, "mp"),
        P("mp"),
        P("mp", None),
        P(),
    )
    return jax.shard_map(
        functools.partial(local, mesh.shape["dp"]), mesh=mesh, in_specs=in_specs, out_specs=out_specs, check_vma=False)
```

```python
import functools

import jax
import jax.numpy as jnp
from jax import lax
from jax.experimental import pallas as pl
from jax.experimental.pallas import tpu as pltpu
from jax.sharding import PartitionSpec as P

HEAD = 64
LANES = 256
TAIL_RADICES = (2,)
epsilon = 1e-06
masked_score = -1e30
low, wide = jnp.bfloat16, jnp.float32
params = pltpu.CompilerParams(vmem_limit_bytes=24 << 20)


def cost(flops, moved, exps=0):
    return pl.CostEstimate(flops=flops, bytes_accessed=moved, transcendentals=exps)


def whole(array):
    return pl.BlockSpec(array.shape, lambda *_: (0,) * len(array.shape))


def shaped(shape, kind):
    return jax.ShapeDtypeStruct(shape, kind)


def mm(left, right, left_dim, right_dim):
    return lax.dot_general(
        left, right, (((left_dim,), (right_dim,)), ((), ())), preferred_element_type=wide
    )


def normalize(values, gain, shift):
    centred = values - jnp.mean(values, axis=-1, keepdims=True)
    spread = jnp.mean(centred * centred, axis=-1, keepdims=True)
    return centred * lax.rsqrt(spread + epsilon) * gain + shift


def normalize_back(values, gain, grad):
    centred = values - jnp.mean(values, axis=-1, keepdims=True)
    inverse = lax.rsqrt(jnp.mean(centred * centred, axis=-1, keepdims=True) + epsilon)
    unit = centred * inverse
    scaled = grad * gain
    by_values = inverse * (
        scaled
        - jnp.mean(scaled, axis=-1, keepdims=True)
        - unit * jnp.mean(scaled * unit, axis=-1, keepdims=True)
    )
    return by_values, jnp.sum(grad * unit, axis=0), jnp.sum(grad, axis=0)


def spans(extent):
    edges = list(range(0, extent, LANES))
    if len(edges) > 1 and extent - edges[-1] < LANES // 2:
        edges.pop()
    return list(zip(edges, edges[1:] + [extent]))


def split_three(row):
    first = row.astype(low).astype(wide)
    second = (row - first).astype(low).astype(wide)
    return first, second, row - first - second


def head_rows(part, width, head):
    return pl.ds(pl.multiple_of(part * width + head * HEAD, HEAD), HEAD)


def project_kernel(
    side_ref, tokens_ref, gain_ref, shift_ref, query_ref, key_ref, value_ref, b_ref, tissue_ref,
    qkv_ref, normed_ref, w_ref, bias_ref
):
    normed = normalize(tokens_ref[...].astype(wide), gain_ref[...][None], shift_ref[...][None]).astype(low)
    normed_ref[...] = normed
    width = query_ref.shape[1]
    for part, ref in enumerate((query_ref, key_ref, value_ref)):
        at = slice(part * width, (part + 1) * width)
        turned = ref[...].T
        w_ref[at] = turned
        qkv_ref[at] = (mm(turned, normed, 1, 1) + b_ref[at]).astype(low)
    own = tokens_ref.shape[0]
    bias = jnp.where(tissue_ref[...] > 0, 0.0, masked_score)
    turned = jnp.concatenate([bias[:, own:], bias[:, :own]], axis=1)
    bias = jnp.where(side_ref[0] == 0, bias, turned)
    index = lax.broadcasted_iota(jnp.int32, bias_ref.shape, 0)
    bias_ref[...] = jnp.where(index == 0, bias, 0.0).astype(low)


def project(side, tokens, gain, shift, w_query, w_key, w_value, b, tissue):
    rows, features = tokens.shape
    width = w_query.shape[1]
    vmem = pl.BlockSpec(memory_space=pltpu.VMEM)
    return pl.pallas_call(
        project_kernel,
        name="project_own_rows",
        in_specs=[pl.BlockSpec(memory_space=pltpu.SMEM)] + [vmem] * 8,
        out_specs=[vmem] * 4,
        out_shape=[
            shaped((3 * width, rows), low),
            shaped((rows, features), low),
            shaped((3 * width, features), low),
            shaped((16, tissue.shape[1]), low),
        ],
        compiler_params=params,
        cost_estimate=cost(10**9, 5 * 10**6),
    )(side, tokens, gain, shift, w_query, w_key, w_value, b, tissue)


def attention_forward_kernel(
    own_ref, own_normed_ref, other_ref, gain_ref, shift_ref, w_ref, b_ref, bias_ref,
    qkv_ref, own_context_ref, other_context_ref, exact_ref, log_ref, normed_ref
):
    head = pl.program_id(0)
    own = other_ref.shape[0]
    rows = 2 * own
    width = w_ref.shape[0] // 3

    @pl.when(head == 0)
    def _():
        normed = normalize(other_ref[...].astype(wide), gain_ref[...][None], shift_ref[...][None]).astype(low)
        normed_ref[:own] = own_normed_ref[...]
        normed_ref[own:] = normed
        for part in range(3):
            at = slice(part * width, (part + 1) * width)
            qkv_ref[at, :own] = own_ref[at]
            qkv_ref[at, own:] = (mm(w_ref[at], normed, 1, 1) + b_ref[at]).astype(low)

    queries = qkv_ref[head_rows(0, width, head)] * jnp.array(HEAD**-0.5, low)
    keys = jnp.concatenate([qkv_ref[head_rows(1, width, head)], bias_ref[...]], axis=0).T
    values = qkv_ref[head_rows(2, width, head)]
    index = lax.broadcasted_iota(jnp.int32, (16, rows), 0)
    queries = jnp.concatenate([queries, jnp.where(index == 0, 1.0, 0.0).astype(low)], axis=0)
    pieces = []
    for start, stop in spans(rows):
        scores = mm(keys, queries[:, start:stop], 1, 0)
        highest = jnp.max(scores, axis=0, keepdims=True)
        powers = jnp.exp(scores - highest)
        total = jnp.sum(powers, axis=0, keepdims=True)
        log_ref[0, :, start:stop] = highest + jnp.log(total)
        pieces.append(mm(values, powers.astype(low), 1, 0) * (1.0 / total))
    context = jnp.concatenate(pieces, axis=1)
    exact_ref[...] = context
    context = context.astype(low)
    own_context_ref[...] = context[:, :own]
    other_context_ref[...] = context[:, own:]


def attention_forward(own, own_normed, other, gain, shift, w, b, bias):
    count, features = other.shape
    width = w.shape[0] // 3
    rows = 2 * count
    by_head = lambda columns: pl.BlockSpec((HEAD, columns), lambda head: (head, 0))
    args = (own, own_normed, other, gain, shift, w, b, bias)
    return pl.pallas_call(
        attention_forward_kernel,
        name="attention_forward",
        grid=(width // HEAD,),
        in_specs=[whole(a) for a in args],
        out_specs=[
            pl.BlockSpec((3 * width, rows), lambda head: (0, 0)),
            by_head(count),
            by_head(count),
            by_head(rows),
            pl.BlockSpec((1, 1, rows), lambda head: (head, 0, 0)),
            pl.BlockSpec((rows, features), lambda head: (0, 0)),
        ],
        out_shape=[
            shaped((3 * width, rows), low),
            shaped((width, count), low),
            shaped((width, count), low),
            shaped((width, rows), wide),
            shaped((width // HEAD, 1, rows), wide),
            shaped((rows, features), low),
        ],
        compiler_params=params,
        cost_estimate=cost(10 * 10**9, 10**7, 4 * 10**6),
    )(*args)


def attention_backward_kernel(qkv_ref, exact_ref, log_ref, bias_ref, own_grad_ref, other_grad_ref, out_ref):
    head = pl.program_id(0)
    rows = qkv_ref.shape[1]
    width = qkv_ref.shape[0] // 3
    scale = HEAD**-0.5
    queries = qkv_ref[head_rows(0, width, head)] * jnp.array(scale, low)
    keys = qkv_ref[head_rows(1, width, head)]
    values = qkv_ref[head_rows(2, width, head)]
    grads = jnp.concatenate([own_grad_ref[...], other_grad_ref[...]], axis=1)
    overlap = jnp.sum(grads.astype(wide) * exact_ref[...], axis=0, keepdims=True)
    index = lax.broadcasted_iota(jnp.int32, (16, rows), 0)

    def stack(top, *extra):
        block = jnp.zeros((16, rows), wide)
        for place, row in enumerate(extra):
            block = jnp.where(index == place, row, block)
        return jnp.concatenate([top, block.astype(low)], axis=0)

    bias = bias_ref[0:1].astype(wide)
    queries_more = stack(queries, 1.0, *split_three(-log_ref[0]))
    keys_more = stack(keys, bias, 1.0, 1.0, 1.0).T
    grads_more = stack(grads, *split_three(-overlap))
    values_more = stack(values, 1.0, 1.0, 1.0).T
    grad_keys = jnp.zeros((HEAD, rows), wide)
    grad_values = jnp.zeros((HEAD, rows), wide)
    for start, stop in spans(rows):
        at = slice(start, stop)
        chances = jnp.exp(mm(keys_more, queries_more[:, at], 1, 0))
        grad_values = grad_values + mm(grads[:, at], chances.astype(low), 1, 1)
        grad_scores = (chances * mm(values_more, grads_more[:, at], 1, 0)).astype(low)
        out_ref[head_rows(0, width, head), at] = (mm(keys, grad_scores, 1, 0) * scale).astype(low)
        grad_keys = grad_keys + mm(queries[:, at], grad_scores, 1, 1)
    out_ref[head_rows(1, width, head)] = grad_keys.astype(low)
    out_ref[head_rows(2, width, head)] = grad_values.astype(low)


def attention_backward(qkv, exact, logs, bias, own_grad, other_grad):
    rows = qkv.shape[1]
    width = qkv.shape[0] // 3
    by_head = lambda columns: pl.BlockSpec((HEAD, columns), lambda head: (head, 0))
    return pl.pallas_call(
        attention_backward_kernel,
        name="attention_backward",
        grid=(width // HEAD,),
        in_specs=[
            whole(qkv),
            by_head(rows),
            pl.BlockSpec((1, 1, rows), lambda head: (head, 0, 0)),
            whole(bias),
            by_head(rows // 2),
            by_head(rows // 2),
        ],
        out_specs=whole(qkv),
        out_shape=shaped(qkv.shape, low),
        compiler_params=params,
        cost_estimate=cost(10 * 10**9, 10**7, 4 * 10**6),
    )(qkv, exact, logs, bias, own_grad, other_grad)


def gelu_both(values):
    below = 0.5 * (1.0 + lax.erf(values * (0.5**0.5)))
    density = jnp.exp(values * values * -0.5) * (2.0 * jnp.pi) ** -0.5
    return values * below, below + values * density


def feed_forward_kernel(
    tokens_ref, mine_ref, peer_ref, w_mine_ref, w_peer_ref, b_ref, gain_ref, shift_ref, cotangent_ref,
    up_ref, b_up_ref, down_ref, *refs, other
):
    if other:
        more, refs = refs[:5], refs[5:]
        hidden_ref, grad_normed_ref, branch_ref, grad_b_ref, grad_up_ref, grad_down_ref, *scratch = refs
        normed_ref, grad_sum, sum_, turned_ref, other_turned_ref = scratch
    else:
        normed_ref, activated_ref, grad_pre_ref, grad_normed_ref, branch_ref, grad_b_ref, grad_sum, sum_ = refs
    step = pl.program_id(0)

    @pl.when(step == 0)
    def _():
        attention = mm(mine_ref[...], w_mine_ref[...], 0, 0) + mm(peer_ref[...], w_peer_ref[...], 0, 0)
        hidden = tokens_ref[...].astype(wide) + (attention + b_ref[...][None])
        normed = normalize(hidden, gain_ref[...][None], shift_ref[...][None]).astype(low)
        normed_ref[...] = normed
        grad_sum[...] = jnp.zeros_like(grad_sum)
        sum_[...] = jnp.zeros_like(sum_)
        if other:
            hidden_ref[...] = hidden
            turned_ref[...] = normed.T
            other_turned_ref[...] = more[0][...].T

    up, down = up_ref[...], down_ref[...]
    pre_gelu = mm(normed_ref[...], up, 1, 0) + b_up_ref[...]
    grad_active = mm(cotangent_ref[...], down, 1, 1)
    activated, slope = gelu_both(pre_gelu)
    activated = activated.astype(low)
    grad_pre = (grad_active * slope).astype(low)
    sums = jnp.sum(grad_pre.astype(wide), axis=0, keepdims=True)
    grad_sum[...] += mm(grad_pre, up, 1, 1)
    sum_[...] += mm(activated, down, 1, 0)
    if other:
        _, other_cotangent_ref, other_activated_ref, other_grad_pre_ref, other_grad_b_ref = more
        grad_b_ref[...] = sums + other_grad_b_ref[...]
        grad_down = mm(activated, cotangent_ref[...], 0, 0)
        grad_down_ref[...] = (grad_down + mm(other_activated_ref[...], other_cotangent_ref[...], 0, 0)).astype(low)
        grad_up = mm(turned_ref[...], grad_pre, 1, 0)
        grad_up_ref[...] = (grad_up + mm(other_turned_ref[...], other_grad_pre_ref[...], 1, 0)).astype(low)
    else:
        grad_b_ref[...] = sums
        activated_ref[...] = activated
        grad_pre_ref[...] = grad_pre

    @pl.when(step == pl.num_programs(0) - 1)
    def _():
        grad_normed_ref[...] = grad_sum[...].astype(low)
        branch_ref[...] = sum_[...].astype(low)


def feed_forward(tokens, mine, peer, w_mine, w_peer, b, gain, shift, cotangent, up, b_up, down, other=()):
    rows, features = tokens.shape
    units = up.shape[1]
    block = 512
    by_rows = pl.BlockSpec((rows, block), lambda step: (0, step))
    by_unit = pl.BlockSpec((1, block), lambda step: (0, step))
    by_up = pl.BlockSpec((features, block), lambda step: (0, step))
    by_down = pl.BlockSpec((block, features), lambda step: (step, 0))
    plain = shaped((rows, features), low)
    scratch = [pltpu.VMEM((rows, features), wide), pltpu.VMEM((rows, features), wide)]
    if other:
        out_specs = [whole(tokens)] * 3 + [by_unit, by_up, by_down]
        out_shape = [shaped((rows, features), wide), plain, plain, shaped((1, units), wide)]
        out_shape += [shaped((features, units), low), shaped((units, features), low)]
        turned = pltpu.VMEM((features, rows), low)
        scratch = [pltpu.VMEM((rows, features), low)] + scratch + [turned, turned]
    else:
        out_specs = [whole(tokens), by_rows, by_rows, whole(tokens), whole(tokens), by_unit]
        out_shape = [plain, shaped((rows, units), low), shaped((rows, units), low), plain, plain]
        out_shape += [shaped((1, units), wide)]
    return pl.pallas_call(
        functools.partial(feed_forward_kernel, other=bool(other)),
        name="feed_forward",
        grid=(units // block,),
        in_specs=[whole(a) for a in (tokens, mine, peer, w_mine, w_peer, b, gain, shift, cotangent)]
        + [by_up, by_unit, by_down]
        + ([whole(other[0]), whole(other[1]), by_rows, by_rows, by_unit] if other else []),
        out_specs=out_specs,
        out_shape=out_shape,
        scratch_shapes=scratch,
        compiler_params=params,
        cost_estimate=cost(5 * 10**9, 10**7, 10**6),
    )(tokens, mine, peer, w_mine, w_peer, b, gain, shift, cotangent, up, b_up, down, *other)


def middle_kernel(
    part_ref, came_ref, hidden_ref, cotangent_ref, gain_ref, w_mine_ref, w_peer_ref,
    grad_hidden_ref, branch_ref, mine_ref, peer_ref, sums_ref
):
    grad = part_ref[...].astype(wide) + came_ref[...].astype(wide)
    cotangent = cotangent_ref[...].astype(wide)
    by_hidden, by_gain, by_shift = normalize_back(hidden_ref[...], gain_ref[...][None], grad)
    grad_hidden = by_hidden + cotangent
    grad_hidden_ref[...] = grad_hidden
    branch = grad_hidden.astype(low)
    branch_ref[...] = branch
    mine_ref[...] = mm(w_mine_ref[...], branch, 1, 1).astype(low)
    peer_ref[...] = mm(w_peer_ref[...], branch, 1, 1).astype(low)
    sums_ref[...] = jnp.zeros_like(sums_ref)
    sums_ref[0:1] = jnp.sum(branch.astype(wide), axis=0, keepdims=True)
    sums_ref[1:2] = by_gain[None]
    sums_ref[2:3] = by_shift[None]
    sums_ref[3:4] = jnp.sum(cotangent, axis=0, keepdims=True)


def middle(part, came, hidden, cotangent, gain, w_mine, w_peer):
    rows, features = part.shape
    width = w_mine.shape[0]
    args = (part, came, hidden, cotangent, gain, w_mine, w_peer)
    return pl.pallas_call(
        middle_kernel,
        name="second_norm_backward",
        out_shape=[
            shaped((rows, features), wide),
            shaped((rows, features), low),
            shaped((width, rows), low),
            shaped((width, rows), low),
            shaped((8, features), wide),
        ],
        compiler_params=params,
        cost_estimate=cost(10**9, 5 * 10**6),
    )(*args)


def last_kernel(
    part_ref, came_ref, tokens_ref, grad_hidden_ref, gain_ref, b_ref, hidden_ref, branch_ref, branch_came_ref,
    out_ref, sums_ref, output_ref
):
    grad = part_ref[...].astype(wide) + came_ref[...].astype(wide)
    by_tokens, by_gain, by_shift = normalize_back(tokens_ref[...].astype(wide), gain_ref[...][None], grad)
    out_ref[...] = grad_hidden_ref[...] + by_tokens
    sums_ref[...] = jnp.zeros_like(sums_ref)
    sums_ref[0:1] = by_gain[None]
    sums_ref[1:2] = by_shift[None]
    branch = branch_ref[...].astype(wide) + branch_came_ref[...].astype(wide)
    output_ref[...] = (hidden_ref[...] + (branch + b_ref[...][None])).astype(low)


def last(part, came, tokens, grad_hidden, gain, b, hidden, branch, branch_came):
    rows, features = part.shape
    return pl.pallas_call(
        last_kernel,
        name="first_norm_backward",
        out_shape=[shaped((rows, features), wide), shaped((8, features), wide), shaped((rows, features), low)],
        compiler_params=params,
        cost_estimate=cost(10**8, 5 * 10**6),
    )(part, came, tokens, grad_hidden, gain, b, hidden, branch, branch_came)


def by_inputs_kernel(grads_ref, w_ref, own_ref, other_ref, sums_ref):
    own = own_ref.shape[0]
    grads = grads_ref[...]
    other_ref[...] = mm(grads[:, own:], w_ref[...], 0, 0).astype(low)
    own_ref[...] = mm(grads[:, :own], w_ref[...], 0, 0).astype(low)
    sums_ref[...] = mm(jnp.ones((8, grads.shape[1]), low), grads, 1, 1)


def by_inputs(grads, w):
    rows, features = grads.shape[1] // 2, w.shape[1]
    return pl.pallas_call(
        by_inputs_kernel,
        name="first_normed_gradient",
        out_shape=[
            shaped((rows, features), low),
            shaped((rows, features), low),
            shaped((8, grads.shape[0]), wide),
        ],
        compiler_params=params,
        cost_estimate=cost(2 * 10**9, 5 * 10**6),
    )(grads, w)


def tail_gradient_kernel(
    core_ref, grads_ref, normed_ref, own_context_ref, own_branch_ref, other_context_ref, other_branch_ref,
    away_ref, kept_ref
):
    step = pl.program_id(0)
    block = tail_block(step, core_ref[0])

    def put(total):
        @pl.when(step < 2)
        def _():
            away_ref[...] = total.astype(low)

        @pl.when(step >= 2)
        def _():
            kept_ref[...] = total

    @pl.when(block < 3)
    def _():
        put(mm(grads_ref[...], normed_ref[...], 1, 0))

    @pl.when(block == 3)
    def _():
        put(
            mm(own_context_ref[...], own_branch_ref[...], 1, 0)
            + mm(other_context_ref[...], other_branch_ref[...], 1, 0)
        )


def tail_block(step, core):
    side = jnp.where(step < 2, 1 - core, core)
    return side * 2 + (step & 1)


def tail_gradient(core, grads, normed, own_context, own_branch, other_context, other_branch):
    width, features = own_context.shape[0], normed.shape[1]
    rest = (normed, own_context, own_branch, other_context, other_branch)
    return pl.pallas_call(
        tail_gradient_kernel,
        name="tail_gradient",
        grid_spec=pltpu.PrefetchScalarGridSpec(
            num_scalar_prefetch=1,
            grid=(4,),
            in_specs=[
                pl.BlockSpec(
                    (width, grads.shape[1]),
                    lambda step, core_ref: (jnp.minimum(tail_block(step, core_ref[0]), 2), 0),
                )
            ]
            + [whole(a) for a in rest],
            out_specs=[
                pl.BlockSpec((width, features), lambda step, _: (jnp.minimum(step, 1), 0)),
                pl.BlockSpec((width, features), lambda step, _: (jnp.maximum(step - 2, 0), 0)),
            ],
        ),
        out_shape=[shaped((2 * width, features), low), shaped((2 * width, features), wide)],
        compiler_params=params,
        cost_estimate=cost(2 * 10**9, 10**7),
    )(core, grads, *rest)


def after(value, *others):
    return lax.optimization_barrier((value, *others))[0]


def swap_mp(value):
    return lax.ppermute(value, "mp", [(0, 1), (1, 0)])


def swap_dp(value, mask, count):
    return lax.ppermute(value, "dp", [(i, i ^ mask) for i in range(count)])


def rows_at(value, at, rows):
    return lax.dynamic_slice_in_dim(value, at * rows, rows, 0)


def rows_set(value, block, at):
    return lax.dynamic_update_slice_in_dim(value, block, at * block.shape[0], 0)


def scatter_sum(block, radix, stride, chip, count):
    digit = (chip // stride) & (radix - 1)
    rows = block.shape[0] // radix
    pieces = [rows_at(block, digit ^ j, rows).astype(low) for j in range(1, radix)]
    total = rows_at(block, digit, rows)
    return total, [swap_dp(piece, 2 * stride * j, count) for j, piece in enumerate(pieces, 1)], pieces


def add_all(total, pieces):
    for piece in pieces:
        total = total + piece.astype(wide)
    return total


def widen(pair):
    rows = pair.shape[0] // 2
    return pair[:rows].astype(wide) + pair[rows:].astype(wide)


def pack_rows(rows):
    top = lax.reduce_precision(rows, exponent_bits=8, mantissa_bits=7)
    return jnp.concatenate([top, rows - top], axis=0).astype(low)


def gather_sum(block, sums, radix, stride, chip, count):
    digit = (chip // stride) & (radix - 1)
    packed = pack_rows(sums)
    extra, rows = packed.shape[0], block.shape[0]
    sent = jnp.concatenate([packed, block], axis=0)
    blocks = {0: block}
    for j in range(1, radix):
        came = swap_dp(sent, 2 * stride * j, count)
        sums = sums + widen(came[:extra])
        blocks[j] = came[extra:]
    orders = [jnp.concatenate([blocks[k ^ d] for k in range(radix)], axis=0) for d in range(radix)]
    whole_block = orders[0]
    for d in range(1, radix):
        whole_block = jnp.where(digit == d, orders[d], whole_block)
    return whole_block, sums


def levels(chips, first):
    out, stride = [], 1
    for radix in first:
        if (chips // stride) % radix == 0:
            out.append((radix, stride))
            stride *= radix
    while stride < chips:
        out.append((2, stride))
        stride *= 2
    return out


def tail_finish_kernel(core_ref, half_ref, came_ref, small_ref, *refs):
    extra = came_ref.shape[0] - half_ref.shape[0]
    rows = extra // 2
    small = small_ref[...] + (came_ref[:rows].astype(wide) + came_ref[rows:extra].astype(wide))
    columns = small.shape[1]
    for row in range(6):
        refs[4 + row][...] = small[row]
    refs[10][...] = small[6, : columns // 2]
    refs[11][...] = small[6, columns // 2 :]
    refs[12][:columns] = small[7]
    refs[12][columns:] = small[8]
    for core in range(2):

        @pl.when(core_ref[0] == core)
        def _():
            width = half_ref.shape[0] // 2
            mine, other = (half_ref, 0), (came_ref, extra)
            (first, at), (second, to) = (mine, other) if core == 0 else (other, mine)
            refs[0][...] = first[at : at + width].astype(wide).T
            refs[1][...] = first[at + width : at + 2 * width].astype(wide).T
            refs[2][...] = second[to : to + width].astype(wide).T
            refs[3][...] = second[to + width : to + 2 * width].astype(wide)


def tail_finish(core, half, came, small):
    rows, features = half.shape
    width = rows // 2
    vmem = pl.BlockSpec(memory_space=pltpu.VMEM)
    vectors = [features] * 6 + [features // 2] * 2 + [2 * features]
    return pl.pallas_call(
        tail_finish_kernel,
        name="tail_finish",
        in_specs=[pl.BlockSpec(memory_space=pltpu.SMEM), vmem, vmem, vmem],
        out_specs=[vmem] * 13,
        out_shape=[shaped((features, width), wide)] * 3
        + [shaped((width, features), wide)]
        + [shaped((n,), wide) for n in vectors],
        compiler_params=params,
        cost_estimate=cost(10**6, 10**7),
    )(core, half, came, small)


def local(
    count,
    tokens,
    tissue,
    first_gain,
    first_shift,
    w_query,
    b_query,
    w_key,
    w_value,
    b_value,
    w_output,
    b_output,
    second_gain,
    second_shift,
    w_upward,
    b_upward,
    w_down,
    b_down,
    cotangent,
):
    place, side = lax.axis_index("dp"), lax.axis_index("mp")
    core = place & 1
    core_list = core.reshape(1)
    own = tokens.shape[0]
    width = w_query.shape[1]
    tokens_other = swap_mp(tokens)
    half_width = width // 2
    w_half = swap_mp(after(rows_at(w_output, core, half_width), tokens_other))
    cotangent_other = swap_mp(after(cotangent, tokens_other))
    b_stack = jnp.concatenate([b_query, jnp.zeros_like(b_query), b_value])[:, None]
    own_qkv, own_normed, w_stack, bias = project(
        side.reshape(1), tokens, first_gain, first_shift, w_query, w_key, w_value, b_stack, tissue
    )

    qkv, own_context, other_context, exact, logs, normed1 = attention_forward(
        own_qkv, own_normed, after(tokens_other, own_qkv), first_gain, first_shift, w_stack, b_stack, bias
    )
    w_traded = swap_dp(after(w_half, own_context), 1, count)
    w_peer = jnp.where(
        core == 0,
        jnp.concatenate([w_half, w_traded], axis=0),
        jnp.concatenate([w_traded, w_half], axis=0),
    )
    peer_own = swap_mp(other_context)
    peer_other = swap_mp(own_context)
    b_up = b_upward[None]
    shared = (w_upward, b_up, w_down)
    second = (b_output, second_gain, second_shift)
    normed_b, active_b, pre_b, part_b, branch_b, sum_b = feed_forward(
        tokens_other, other_context, peer_other, w_output, w_peer, *second, cotangent_other, *shared
    )
    came = swap_mp(part_b)
    hidden, part_a, branch_a, grad_bupward, grad_upward, grad_down = feed_forward(
        after(tokens, part_b), own_context, peer_own, w_output, w_peer, *second, cotangent, *shared,
        other=(normed_b, cotangent_other, active_b, pre_b, sum_b),
    )
    sum_down, sum_upward = lax.psum((grad_down, grad_upward), "dp")

    grad_hidden, grad_branch, mine_own, peer_grad, sums = middle(
        part_a, came, after(hidden, grad_down), cotangent, second_gain, w_output, w_peer
    )
    mine_other = swap_mp(peer_grad)

    def rest(mine_own, mine_other):
        chip = place >> 1
        steps = levels(count // 2, TAIL_RADICES)
        branch_other = swap_mp(after(grad_branch, mine_other))
        branch_came = swap_mp(after(branch_b, mine_other))
        grads = attention_backward(qkv, exact, logs, bias, mine_own, mine_other)
        away, kept = tail_gradient(
            core_list, grads, normed1, own_context, grad_branch, other_context, branch_other
        )
        half = kept + swap_dp(away, 1, count).astype(wide)
        total, arrived, sent = scatter_sum(half, *steps[0], chip, count)
        first_a, first_b, stack_sums = by_inputs(after(grads, branch_came, *sent), w_stack)
        came = swap_mp(first_b)
        half = add_all(total, arrived)
        for step in steps[1:]:
            total, arrived, sent = scatter_sum(half, *step, chip, count)
            half = add_all(total, arrived)
        half = half.astype(low)
        grad_tokens, sums_first, output = last(
            first_a, came, tokens, grad_hidden, first_gain, b_down, hidden, branch_a, branch_came
        )

        shared = jnp.concatenate([sums_first[:2], sums[:4]], axis=0)
        shared = shared + swap_mp(shared)
        columns = shared.shape[1]
        split = jnp.concatenate([stack_sums[0, :width], stack_sums[0, 2 * width :], grad_bupward[0]])
        small = jnp.concatenate([shared, split.reshape(-1, columns)], axis=0)
        small = jnp.pad(small, ((0, -small.shape[0] % 4), (0, 0)))
        for step in reversed(steps):
            half, small = gather_sum(half, small, *step, chip, count)
        came = swap_dp(jnp.concatenate([pack_rows(small), half], axis=0), 1, count)
        return (output, grad_tokens, *tail_finish(core_list, half, came, small))

    def none(mine_own, mine_other):
        return jax.tree.map(lambda a: jnp.zeros(a.shape, a.dtype), jax.eval_shape(rest, mine_own, mine_other))

    output, grad_tokens, grad_wquery, grad_wkey, grad_wvalue, grad_woutput, *small = lax.cond(
        tissue[0, 0] >= 0, rest, none, after(mine_own, grad_upward), mine_other
    )
    return (
        output,
        grad_tokens,
        small[0],
        small[1],
        grad_wquery,
        small[6],
        grad_wkey,
        grad_wvalue,
        small[7],
        grad_woutput,
        small[2],
        small[3],
        small[4],
        sum_upward.astype(wide),
        small[8],
        sum_down.astype(wide),
        small[5],
    )


def solution(mesh):
    in_specs = (
        P(("dp", "mp"), None),
        P("dp", None),
        P(),
        P(),
        P(None, "mp"),
        P("mp"),
        P(None, "mp"),
        P(None, "mp"),
        P("mp"),
        P("mp", None),
        P(),
        P(),
        P(),
        P(None, "mp"),
        P("mp"),
        P("mp", None),
        P(),
        P(("dp", "mp"), None),
    )
    out_specs = (
        P(("dp", "mp"), None),
        P(("dp", "mp"), None),
        P(),
        P(),
        P(None, "mp"),
        P("mp"),
        P(None, "mp"),
        P(None, "mp"),
        P("mp"),
        P("mp", None),
        P(),
        P(),
        P(),
        P(None, "mp"),
        P("mp"),
        P("mp", None),
        P(),
    )
    return jax.shard_map(
        functools.partial(local, mesh.shape["dp"]), mesh=mesh, in_specs=in_specs, out_specs=out_specs, check_vma=False)
```

```python
import functools

import jax
import jax.numpy as jnp
from jax import lax
from jax.experimental import pallas as pl
from jax.experimental.pallas import tpu as pltpu
from jax.sharding import PartitionSpec as P

HEAD = 64
GROUP = 3
BLOCK = 512
epsilon = 1e-06
masked_score = -1e30
low, wide = jnp.bfloat16, jnp.float32
params = pltpu.CompilerParams(vmem_limit_bytes=24 << 20)


def cost(flops, moved, exps=0):
    return pl.CostEstimate(flops=flops, bytes_accessed=moved, transcendentals=exps)


def whole(array):
    return pl.BlockSpec(array.shape, lambda *_: (0,) * len(array.shape))


def shaped(shape, kind):
    return jax.ShapeDtypeStruct(shape, kind)


def stored(shape, kind):
    return pltpu.HBM(shape, kind)


def ordered_call(
    kernel, args, in_specs, out_specs, out_shape, behind=(), through=(), prefetch=0, grid=(), scratch=(), **rest
):
    count, outputs = len(args), len(out_shape)
    skipped = len(behind) + len(through)
    place = pl.BlockSpec(memory_space=pl.ANY)

    def body(*refs):
        given, refs = refs[:count], refs[count + skipped :]
        kernel(*given, *refs[:outputs], *refs[outputs + len(through) :])

    first = count + len(behind)
    out = pl.pallas_call(
        body,
        grid_spec=pltpu.PrefetchScalarGridSpec(
            num_scalar_prefetch=prefetch,
            grid=grid,
            in_specs=list(in_specs) + [place] * skipped,
            out_specs=list(out_specs) + [place] * len(through),
            scratch_shapes=list(scratch),
        ),
        out_shape=list(out_shape) + [shaped(a.shape, a.dtype) for a in through],
        input_output_aliases={first + k: outputs + k for k in range(len(through))},
        compiler_params=params,
        **rest,
    )(*args, *behind, *through)
    return list(out[:outputs]), list(out[outputs:])


def far(array):
    return pltpu.with_memory_space_constraint(array, pltpu.HBM)


def mm(left, right, left_dim, right_dim):
    return lax.dot_general(
        left, right, (((left_dim,), (right_dim,)), ((), ())), preferred_element_type=wide
    )


def normalize(values, gain, shift):
    centred = values - jnp.mean(values, axis=-1, keepdims=True)
    spread = jnp.mean(centred * centred, axis=-1, keepdims=True)
    return centred * lax.rsqrt(spread + epsilon) * gain + shift


def normalize_back(values, gain, grad):
    centred = values - jnp.mean(values, axis=-1, keepdims=True)
    inverse = lax.rsqrt(jnp.mean(centred * centred, axis=-1, keepdims=True) + epsilon)
    unit = centred * inverse
    scaled = grad * gain
    by_values = inverse * (
        scaled
        - jnp.mean(scaled, axis=-1, keepdims=True)
        - unit * jnp.mean(scaled * unit, axis=-1, keepdims=True)
    )
    return by_values, jnp.sum(grad * unit, axis=0), jnp.sum(grad, axis=0)


def split_three(row):
    first = row.astype(low).astype(wide)
    second = (row - first).astype(low).astype(wide)
    return first, second, row - first - second


def head_rows(part, width, head):
    return pl.ds(pl.multiple_of(part * width + head * HEAD, HEAD), HEAD)


def project_kernel(
    side_ref, tokens_ref, gain_ref, shift_ref, query_ref, key_ref, value_ref, b_ref, tissue_ref,
    qkv_ref, normed_ref, w_ref, bias_ref
):
    normed = normalize(tokens_ref[...].astype(wide), gain_ref[...][None], shift_ref[...][None]).astype(low)
    normed_ref[...] = normed
    width = query_ref.shape[1]
    for part, ref in enumerate((query_ref, key_ref, value_ref)):
        at = slice(part * width, (part + 1) * width)
        turned = ref[...].T
        w_ref[at] = turned
        qkv_ref[at] = (mm(turned, normed, 1, 1) + b_ref[at]).astype(low)
    own = tokens_ref.shape[0]
    bias = jnp.where(tissue_ref[...] > 0, 0.0, masked_score)
    turned = jnp.concatenate([bias[:, own:], bias[:, :own]], axis=1)
    bias = jnp.where(side_ref[0] == 0, bias, turned)
    index = lax.broadcasted_iota(jnp.int32, bias_ref.shape, 0)
    bias_ref[...] = jnp.where(index == 0, bias, 0.0).astype(low)


def project(side, tokens, gain, shift, w_query, w_key, w_value, b, tissue):
    rows, features = tokens.shape
    width = w_query.shape[1]
    vmem = pl.BlockSpec(memory_space=pltpu.VMEM)
    return pl.pallas_call(
        project_kernel,
        name="project_own_rows",
        in_specs=[pl.BlockSpec(memory_space=pltpu.SMEM)] + [vmem] * 8,
        out_specs=[vmem] * 4,
        out_shape=[
            shaped((3 * width, rows), low),
            shaped((rows, features), low),
            shaped((3 * width, features), low),
            shaped((16, tissue.shape[1]), low),
        ],
        compiler_params=params,
        cost_estimate=cost(10**9, 5 * 10**6),
    )(side, tokens, gain, shift, w_query, w_key, w_value, b, tissue)


def attention_forward_kernel(
    own_ref, own_normed_ref, other_ref, gain_ref, shift_ref, w_ref, b_ref, bias_ref,
    qkv_ref, own_context_ref, other_context_ref, exact_ref, log_ref, normed_ref
):
    group = pl.program_id(0)
    own = other_ref.shape[0]
    rows = 2 * own
    width = w_ref.shape[0] // 3

    @pl.when(group == 0)
    def _():
        normed = normalize(other_ref[...].astype(wide), gain_ref[...][None], shift_ref[...][None]).astype(low)
        normed_ref[:own] = own_normed_ref[...]
        normed_ref[own:] = normed
        for part in range(3):
            at = slice(part * width, (part + 1) * width)
            qkv_ref[at, :own] = own_ref[at]
            qkv_ref[at, own:] = (mm(w_ref[at], normed, 1, 1) + b_ref[at]).astype(low)

    index = lax.broadcasted_iota(jnp.int32, (16, rows), 0)
    ones = jnp.where(index == 0, 1.0, 0.0).astype(low)
    for local_head in range(GROUP):
        head = group * GROUP + local_head
        queries = qkv_ref[head_rows(0, width, head)] * jnp.array(HEAD**-0.5, low)
        keys = jnp.concatenate([qkv_ref[head_rows(1, width, head)], bias_ref[...]], axis=0).T
        values = qkv_ref[head_rows(2, width, head)]
        scores = mm(keys, jnp.concatenate([queries, ones], axis=0), 1, 0)
        highest = jnp.max(scores, axis=0, keepdims=True)
        powers = jnp.exp(scores - highest)
        total = jnp.sum(powers, axis=0, keepdims=True)
        log_ref[local_head] = highest + jnp.log(total)
        context = mm(values, powers.astype(low), 1, 0) * (1.0 / total)
        at = slice(local_head * HEAD, (local_head + 1) * HEAD)
        exact_ref[at] = context
        context = context.astype(low)
        own_context_ref[at] = context[:, :own]
        other_context_ref[at] = context[:, own:]


def attention_forward(own, own_normed, other, gain, shift, w, b, bias):
    count, features = other.shape
    width = w.shape[0] // 3
    rows = 2 * count
    by_head = lambda columns: pl.BlockSpec((GROUP * HEAD, columns), lambda group: (group, 0))
    args = (own, own_normed, other, gain, shift, w, b, bias)
    return pl.pallas_call(
        attention_forward_kernel,
        name="attention_forward",
        grid=(width // HEAD // GROUP,),
        in_specs=[whole(a) for a in args],
        out_specs=[
            pl.BlockSpec((3 * width, rows), lambda group: (0, 0)),
            by_head(count),
            by_head(count),
            by_head(rows),
            pl.BlockSpec((GROUP, 1, rows), lambda group: (group, 0, 0)),
            pl.BlockSpec((rows, features), lambda group: (0, 0)),
        ],
        out_shape=[
            stored((3 * width, rows), low),
            shaped((width, count), low),
            shaped((width, count), low),
            stored((width, rows), wide),
            shaped((width // HEAD, 1, rows), wide),
            stored((rows, features), low),
        ],
        compiler_params=params,
        cost_estimate=cost(10 * 10**9, 10**7, 4 * 10**6),
    )(*args)


def attention_backward_kernel(qkv_ref, exact_ref, log_ref, bias_ref, own_grad_ref, other_grad_ref, out_ref):
    rows = qkv_ref.shape[1]
    width = qkv_ref.shape[0] // 3
    scale = HEAD**-0.5
    index = lax.broadcasted_iota(jnp.int32, (16, rows), 0)

    def stack(top, *extra):
        block = jnp.zeros((16, rows), wide)
        for place, row in enumerate(extra):
            block = jnp.where(index == place, row, block)
        return jnp.concatenate([top, block.astype(low)], axis=0)

    bias = bias_ref[0:1].astype(wide)
    for local_head in range(GROUP):
        head = pl.program_id(0) * GROUP + local_head
        at = slice(local_head * HEAD, (local_head + 1) * HEAD)
        queries = qkv_ref[head_rows(0, width, head)] * jnp.array(scale, low)
        keys = qkv_ref[head_rows(1, width, head)]
        values = qkv_ref[head_rows(2, width, head)]
        grads = jnp.concatenate([own_grad_ref[at], other_grad_ref[at]], axis=1)
        overlap = jnp.sum(grads.astype(wide) * exact_ref[at], axis=0, keepdims=True)
        queries_more = stack(queries, 1.0, *split_three(-log_ref[local_head]))
        keys_more = stack(keys, bias, 1.0, 1.0, 1.0).T
        grads_more = stack(grads, *split_three(-overlap))
        values_more = stack(values, 1.0, 1.0, 1.0).T
        chances = jnp.exp(mm(keys_more, queries_more, 1, 0))
        out_ref[head_rows(2, width, head)] = mm(grads, chances.astype(low), 1, 1).astype(low)
        grad_scores = (chances * mm(values_more, grads_more, 1, 0)).astype(low)
        out_ref[head_rows(0, width, head)] = (mm(keys, grad_scores, 1, 0) * scale).astype(low)
        out_ref[head_rows(1, width, head)] = mm(queries, grad_scores, 1, 1).astype(low)


def attention_backward(qkv, exact, logs, bias, own_grad, other_grad, behind, through):
    rows = qkv.shape[1]
    width = qkv.shape[0] // 3
    by_head = lambda columns: pl.BlockSpec((GROUP * HEAD, columns), lambda group: (group, 0))
    return ordered_call(
        attention_backward_kernel,
        (qkv, exact, logs, bias, own_grad, other_grad),
        [
            whole(qkv),
            by_head(rows),
            pl.BlockSpec((GROUP, 1, rows), lambda group: (group, 0, 0)),
            whole(bias),
            by_head(rows // 2),
            by_head(rows // 2),
        ],
        [whole(qkv)],
        [shaped(qkv.shape, low)],
        behind=behind,
        through=through,
        grid=(width // HEAD // GROUP,),
        name="attention_backward",
        cost_estimate=cost(10 * 10**9, 10**7, 4 * 10**6),
    )


def gelu_both(values):
    below = 0.5 * (1.0 + lax.erf(values * (0.5**0.5)))
    density = jnp.exp(values * values * -0.5) * (2.0 * jnp.pi) ** -0.5
    return values * below, below + values * density


def feed_forward_kernel(
    tokens_ref, mine_ref, peer_ref, w_mine_ref, w_peer_ref, b_ref, gain_ref, shift_ref, cotangent_ref,
    up_ref, b_up_ref, down_ref, *refs, other
):
    if other:
        core_ref, *more = refs[:6]
        hidden_ref, grad_normed_ref, branch_ref, grad_b_ref, away_ref, kept_ref, *scratch = refs[6:]
        normed_ref, grad_sum, sum_ = scratch
    else:
        normed_ref, activated_ref, grad_pre_ref, grad_normed_ref, branch_ref, grad_b_ref, grad_sum, sum_ = refs
    step = pl.program_id(0)

    @pl.when(step == 0)
    def _():
        attention = mm(mine_ref[...], w_mine_ref[...], 0, 0) + mm(peer_ref[...], w_peer_ref[...], 0, 0)
        hidden = tokens_ref[...].astype(wide) + (attention + b_ref[...][None])
        normed = normalize(hidden, gain_ref[...][None], shift_ref[...][None]).astype(low)
        normed_ref[...] = normed
        grad_sum[...] = jnp.zeros_like(grad_sum)
        sum_[...] = jnp.zeros_like(sum_)
        if other:
            hidden_ref[...] = hidden

    up, down = up_ref[...], down_ref[...]
    pre_gelu = mm(normed_ref[...], up, 1, 0) + b_up_ref[...]
    grad_active = mm(cotangent_ref[...], down, 1, 1)
    activated, slope = gelu_both(pre_gelu)
    activated = activated.astype(low)
    grad_pre = (grad_active * slope).astype(low)
    sums = jnp.sum(grad_pre.astype(wide), axis=0, keepdims=True)
    grad_sum[...] += mm(grad_pre, up, 1, 1)
    sum_[...] += mm(activated, down, 1, 0)
    if other:
        other_normed_ref, other_cotangent_ref, other_activated_ref, other_grad_pre_ref, other_grad_b_ref = more
        grad_b_ref[...] = sums + other_grad_b_ref[...]
        grad_down = mm(activated, cotangent_ref[...], 0, 0)
        grad_down = (grad_down + mm(other_activated_ref[...], other_cotangent_ref[...], 0, 0)).astype(low)
        grad_up = mm(grad_pre, normed_ref[...], 0, 0)
        grad_up = (grad_up + mm(other_grad_pre_ref[...], other_normed_ref[...], 0, 0)).astype(low)
        is_first = core_ref[0] == 0
        away_ref[...] = jnp.where(is_first, grad_up, grad_down)
        kept_ref[...] = jnp.where(is_first, grad_down, grad_up)
    else:
        grad_b_ref[...] = sums
        activated_ref[...] = activated
        grad_pre_ref[...] = grad_pre

    @pl.when(step == pl.num_programs(0) - 1)
    def _():
        grad_normed_ref[...] = grad_sum[...].astype(low)
        branch_ref[...] = sum_[...].astype(low)


def feed_forward(tokens, mine, peer, w_mine, w_peer, b, gain, shift, cotangent, up, b_up, down, other=()):
    rows, features = tokens.shape
    units = up.shape[1]
    block = BLOCK
    by_rows = pl.BlockSpec((rows, block), lambda step: (0, step))
    by_unit = pl.BlockSpec((1, block), lambda step: (0, step))
    by_up = pl.BlockSpec((features, block), lambda step: (0, step))
    by_down = pl.BlockSpec((block, features), lambda step: (step, 0))
    plain = shaped((rows, features), low)
    scratch = [pltpu.VMEM((rows, features), wide), pltpu.VMEM((rows, features), wide)]
    if other:
        out_specs = [whole(tokens)] * 3 + [by_unit, by_down, by_down]
        out_shape = [stored((rows, features), wide), plain, stored((rows, features), low), shaped((1, units), wide)]
        out_shape += [stored((units, features), low)] * 2
        scratch = [pltpu.VMEM((rows, features), low)] + scratch
    else:
        out_specs = [whole(tokens), by_rows, by_rows, whole(tokens), whole(tokens), by_unit]
        out_shape = [plain, shaped((rows, units), low), shaped((rows, units), low), plain]
        out_shape += [stored((rows, features), low)]
        out_shape += [shaped((1, units), wide)]
    return pl.pallas_call(
        functools.partial(feed_forward_kernel, other=bool(other)),
        name="feed_forward",
        grid=(units // block,),
        in_specs=[whole(a) for a in (tokens, mine, peer, w_mine, w_peer, b, gain, shift, cotangent)]
        + [by_up, by_unit, by_down]
        + (
            [pl.BlockSpec(memory_space=pltpu.SMEM), whole(other[1]), whole(other[2]), by_rows, by_rows, by_unit]
            if other
            else []
        ),
        out_specs=out_specs,
        out_shape=out_shape,
        scratch_shapes=scratch,
        compiler_params=params,
        cost_estimate=cost(5 * 10**9, 10**7, 10**6),
    )(tokens, mine, peer, w_mine, w_peer, b, gain, shift, cotangent, up, b_up, down, *other)


def middle_kernel(
    part_ref, came_ref, hidden_ref, cotangent_ref, gain_ref, w_mine_ref, w_peer_ref,
    grad_hidden_ref, branch_ref, mine_ref, peer_ref, sums_ref
):
    grad = part_ref[...].astype(wide) + came_ref[...].astype(wide)
    cotangent = cotangent_ref[...].astype(wide)
    by_hidden, by_gain, by_shift = normalize_back(hidden_ref[...], gain_ref[...][None], grad)
    grad_hidden = by_hidden + cotangent
    grad_hidden_ref[...] = grad_hidden
    branch = grad_hidden.astype(low)
    branch_ref[...] = branch
    mine_ref[...] = mm(w_mine_ref[...], branch, 1, 1).astype(low)
    peer_ref[...] = mm(w_peer_ref[...], branch, 1, 1).astype(low)
    sums_ref[...] = jnp.zeros_like(sums_ref)
    sums_ref[0:1] = jnp.sum(branch.astype(wide), axis=0, keepdims=True)
    sums_ref[1:2] = by_gain[None]
    sums_ref[2:3] = by_shift[None]
    sums_ref[3:4] = jnp.sum(cotangent, axis=0, keepdims=True)


def middle(part, came, hidden, cotangent, gain, w_mine, w_peer, through):
    rows, features = part.shape
    width = w_mine.shape[0]
    vmem = pl.BlockSpec(memory_space=pltpu.VMEM)
    return ordered_call(
        middle_kernel,
        (part, came, hidden, cotangent, gain, w_mine, w_peer),
        [vmem] * 7,
        [vmem] * 5,
        [
            stored((rows, features), wide),
            stored((rows, features), low),
            stored((width, rows), low),
            stored((width, rows), low),
            shaped((8, features), wide),
        ],
        through=through,
        name="second_norm_backward",
        cost_estimate=cost(10**9, 5 * 10**6),
    )


def last_kernel(
    part_ref, came_ref, tokens_ref, grad_hidden_ref, gain_ref, b_ref, hidden_ref, branch_ref, branch_came_ref,
    out_ref, sums_ref, output_ref
):
    grad = part_ref[...].astype(wide) + came_ref[...].astype(wide)
    by_tokens, by_gain, by_shift = normalize_back(tokens_ref[...].astype(wide), gain_ref[...][None], grad)
    out_ref[...] = grad_hidden_ref[...] + by_tokens
    sums_ref[...] = jnp.zeros_like(sums_ref)
    sums_ref[0:1] = by_gain[None]
    sums_ref[1:2] = by_shift[None]
    branch = branch_ref[...].astype(wide) + branch_came_ref[...].astype(wide)
    output_ref[...] = (hidden_ref[...] + (branch + b_ref[...][None])).astype(low)


def last(part, came, tokens, grad_hidden, gain, b, hidden, branch, branch_came, behind, through):
    rows, features = part.shape
    vmem = pl.BlockSpec(memory_space=pltpu.VMEM)
    return ordered_call(
        last_kernel,
        (part, came, tokens, grad_hidden, gain, b, hidden, branch, branch_came),
        [vmem] * 9,
        [vmem] * 3,
        [shaped((rows, features), wide), shaped((8, features), wide), shaped((rows, features), low)],
        behind=behind,
        through=through,
        name="first_norm_backward",
        cost_estimate=cost(10**8, 5 * 10**6),
    )


def by_inputs_kernel(grads_ref, w_ref, own_ref, other_ref, sums_ref):
    own = own_ref.shape[0]
    grads = grads_ref[...]
    other_ref[...] = mm(grads[:, own:], w_ref[...], 0, 0).astype(low)
    own_ref[...] = mm(grads[:, :own], w_ref[...], 0, 0).astype(low)
    sums_ref[...] = mm(jnp.ones((8, grads.shape[1]), low), grads, 1, 1)


def by_inputs(grads, w, behind, through):
    rows, features = grads.shape[1] // 2, w.shape[1]
    vmem = pl.BlockSpec(memory_space=pltpu.VMEM)
    return ordered_call(
        by_inputs_kernel,
        (grads, w),
        [vmem] * 2,
        [vmem] * 3,
        [
            stored((rows, features), low),
            stored((rows, features), low),
            shaped((8, grads.shape[0]), wide),
        ],
        behind=behind,
        through=through,
        name="first_normed_gradient",
        cost_estimate=cost(2 * 10**9, 5 * 10**6),
    )


def tail_gradient_kernel(
    core_ref, grads_ref, normed_ref, own_context_ref, own_branch_ref, other_context_ref, other_branch_ref,
    away_ref, kept_ref
):
    step = pl.program_id(0)
    block = tail_block(step, core_ref[0])

    def put(total):
        @pl.when(step < 2)
        def _():
            away_ref[...] = total.astype(low)

        @pl.when(step >= 2)
        def _():
            kept_ref[...] = total

    @pl.when(block < 3)
    def _():
        put(mm(grads_ref[...], normed_ref[...], 1, 0))

    @pl.when(block == 3)
    def _():
        put(
            mm(own_context_ref[...], own_branch_ref[...], 1, 0)
            + mm(other_context_ref[...], other_branch_ref[...], 1, 0)
        )


def tail_block(step, core):
    side = jnp.where(step < 2, 1 - core, core)
    return side * 2 + (step & 1)


def tail_gradient(core, grads, normed, own_context, own_branch, other_context, other_branch, behind):
    width, features = own_context.shape[0], normed.shape[1]
    rest = (normed, own_context, own_branch, other_context, other_branch)
    return ordered_call(
        tail_gradient_kernel,
        (core, grads, *rest),
        [
            pl.BlockSpec(
                (width, grads.shape[1]),
                lambda step, core_ref: (jnp.minimum(tail_block(step, core_ref[0]), 2), 0),
            )
        ]
        + [whole(a) for a in rest],
        [
            pl.BlockSpec((width, features), lambda step, _: (jnp.minimum(step, 1), 0)),
            pl.BlockSpec((width, features), lambda step, _: (jnp.maximum(step - 2, 0), 0)),
        ],
        [stored((2 * width, features), low), stored((2 * width, features), wide)],
        behind=behind,
        prefetch=1,
        grid=(4,),
        name="tail_gradient",
        cost_estimate=cost(2 * 10**9, 10**7),
    )[0]


def after(value, *others):
    return lax.optimization_barrier((value, *others))[0]


def swap_mp(value):
    return lax.ppermute(value, "mp", [(0, 1), (1, 0)])


def swap_dp(value, mask, count):
    return lax.ppermute(value, "dp", [(i, i ^ mask) for i in range(count)])


def rows_at(value, at, rows):
    return lax.dynamic_slice_in_dim(value, at * rows, rows, 0)


def rows_set(value, block, at):
    return lax.dynamic_update_slice_in_dim(value, block, at * block.shape[0], 0)


class Sum:
    def __init__(self, kept, came, place, count):
        self.count, self.rows = count, kept.shape[0]
        self.terms, self.came = [(kept, 0)], came
        self.core, chip = place & 1, place >> 1
        bits = (count // 2).bit_length() - 1
        self.orders = [(k, (k + 1) % bits) for k in range(bits)]
        self.bits = [(chip >> jnp.where(self.core == 0, a, b)) & 1 for a, b in self.orders]
        self.sums = None

    def swap(self, value, step):
        partner = lambda i: i ^ (2 << self.orders[step][i & 1])
        return lax.ppermute(value, "dp", [(i, partner(i)) for i in range(self.count)])

    def rows_of(self, shift, rows):
        total = 0.0
        for array, start in self.terms:
            total = total + lax.dynamic_slice_in_dim(array, start + shift, rows, 0).astype(wide)
        return total.astype(low)

    def scatter(self, step):
        self.terms.append((self.came, 0))
        self.rows //= 2
        sent = self.rows_of((1 - self.bits[step]) * self.rows, self.rows)
        self.came = self.swap(sent, step)
        self.terms = [(array, start + self.bits[step] * self.rows) for array, start in self.terms]
        return sent

    def turn(self, sums=None):
        self.terms.append((self.came, 0))
        self.block = self.rows_of(0, self.rows)
        self.sums = sums
        return self.send(len(self.orders) - 1)

    def send(self, step):
        sent = self.block if self.sums is None else jnp.concatenate([pack_rows(self.sums), self.block], axis=0)
        self.came = self.swap(sent, step) if step >= 0 else swap_dp(sent, 1, self.count)
        return sent

    def gather(self, step):
        came = self.came
        extra = came.shape[0] - self.block.shape[0]
        if extra:
            self.sums = self.sums + widen(came[:extra])
        mine, other = self.block, came[extra:]
        self.block = jnp.where(
            self.bits[step] == 0,
            jnp.concatenate([mine, other], axis=0),
            jnp.concatenate([other, mine], axis=0),
        )
        return self.send(step - 1)


def widen(pair):
    rows = pair.shape[0] // 2
    return pair[:rows].astype(wide) + pair[rows:].astype(wide)


def pack_rows(rows):
    top = lax.reduce_precision(rows, exponent_bits=8, mantissa_bits=7)
    return jnp.concatenate([top, rows - top], axis=0).astype(low)


def up_down_finish_kernel(core_ref, mine_ref, other_ref, up_ref, down_ref):
    for core in range(2):

        @pl.when(core_ref[0] == core)
        def _():
            down, up = (mine_ref, other_ref) if core == 0 else (other_ref, mine_ref)
            down_ref[...] = down[...].astype(wide)
            up_ref[...] = up[...].astype(wide).T


def up_down_finish(core, mine, other):
    units, features = mine.shape
    block = 256
    by_unit = pl.BlockSpec((block, features), lambda step: (step, 0))
    return pl.pallas_call(
        up_down_finish_kernel,
        name="up_down_finish",
        grid=(units // block,),
        in_specs=[pl.BlockSpec(memory_space=pltpu.SMEM), by_unit, by_unit],
        out_specs=[pl.BlockSpec((features, block), lambda step: (0, step)), by_unit],
        out_shape=[shaped((features, units), wide), shaped((units, features), wide)],
        compiler_params=params,
        cost_estimate=cost(10**6, 10**7),
    )(core, mine, other)


def tail_finish_kernel(core_ref, half_ref, came_ref, small_ref, *refs):
    extra = came_ref.shape[0] - half_ref.shape[0]
    rows = extra // 2
    small = small_ref[...] + (came_ref[:rows].astype(wide) + came_ref[rows:extra].astype(wide))
    columns = small.shape[1]
    for row in range(6):
        refs[4 + row][...] = small[row]
    refs[10][...] = small[6, : columns // 2]
    refs[11][...] = small[6, columns // 2 :]
    refs[12][:columns] = small[7]
    refs[12][columns:] = small[8]
    for core in range(2):

        @pl.when(core_ref[0] == core)
        def _():
            width = half_ref.shape[0] // 2
            mine, other = (half_ref, 0), (came_ref, extra)
            (first, at), (second, to) = (mine, other) if core == 0 else (other, mine)
            refs[0][...] = first[at : at + width].astype(wide).T
            refs[1][...] = first[at + width : at + 2 * width].astype(wide).T
            refs[2][...] = second[to : to + width].astype(wide).T
            refs[3][...] = second[to + width : to + 2 * width].astype(wide)


def tail_finish(core, half, came, small):
    rows, features = half.shape
    width = rows // 2
    vmem = pl.BlockSpec(memory_space=pltpu.VMEM)
    vectors = [features] * 6 + [features // 2] * 2 + [2 * features]
    return pl.pallas_call(
        tail_finish_kernel,
        name="tail_finish",
        in_specs=[pl.BlockSpec(memory_space=pltpu.SMEM), vmem, vmem, vmem],
        out_specs=[vmem] * 13,
        out_shape=[shaped((features, width), wide)] * 3
        + [shaped((width, features), wide)]
        + [shaped((n,), wide) for n in vectors],
        compiler_params=params,
        cost_estimate=cost(10**6, 10**7),
    )(core, half, came, small)


def local(
    count,
    tokens,
    tissue,
    first_gain,
    first_shift,
    w_query,
    b_query,
    w_key,
    w_value,
    b_value,
    w_output,
    b_output,
    second_gain,
    second_shift,
    w_upward,
    b_upward,
    w_down,
    b_down,
    cotangent,
):
    place, side = lax.axis_index("dp"), lax.axis_index("mp")
    core = place & 1
    core_list = core.reshape(1)
    own = tokens.shape[0]
    width = w_query.shape[1]
    tokens_other = swap_mp(tokens)
    half_width = width // 2
    w_half = swap_mp(after(rows_at(w_output, core, half_width), tokens_other))
    cotangent_other = swap_mp(after(cotangent, tokens_other))
    b_stack = jnp.concatenate([b_query, jnp.zeros_like(b_query), b_value])[:, None]
    own_qkv, own_normed, w_stack, bias = project(
        side.reshape(1), tokens, first_gain, first_shift, w_query, w_key, w_value, b_stack, tissue
    )

    qkv, own_context, other_context, exact, logs, normed1 = attention_forward(
        own_qkv, own_normed, after(tokens_other, own_qkv), first_gain, first_shift, w_stack, b_stack, bias
    )
    w_traded = swap_dp(after(w_half, own_context), 1, count)
    w_peer = jnp.where(
        core == 0,
        jnp.concatenate([w_half, w_traded], axis=0),
        jnp.concatenate([w_traded, w_half], axis=0),
    )
    peer_other = swap_mp(own_context)
    peer_own = swap_mp(after(other_context, peer_other))
    b_up = b_upward[None]
    shared = (far(w_upward), b_up, far(w_down))
    second = (b_output, second_gain, second_shift)
    normed_b, active_b, pre_b, part_b, branch_b, sum_b = feed_forward(
        tokens_other, other_context, peer_other, w_output, w_peer, *second, cotangent_other, *shared
    )
    came = swap_mp(part_b)
    hidden, part_a, branch_a, grad_bupward, up_down_away, up_down_kept = feed_forward(
        after(tokens, part_b), own_context, peer_own, w_output, w_peer, *second, cotangent, *shared,
        other=(core_list, normed_b, cotangent_other, active_b, pre_b, sum_b),
    )
    (grad_hidden, grad_branch, mine_own, peer_grad, sums), (up_down_away,) = middle(
        part_a, came, hidden, cotangent, second_gain, w_output, w_peer, through=(up_down_away,)
    )
    up_down = Sum(up_down_kept, swap_dp(up_down_away, 1, count), place, count)
    mine_other = swap_mp(peer_grad)
    branch_other = swap_mp(after(grad_branch, mine_other))
    step = up_down.scatter(0)
    (grads,), (branch_b, *arrays) = attention_backward(
        far(qkv), far(exact), logs, bias, mine_own, mine_other, behind=(step,), through=(branch_b, up_down.terms[0][0])
    )
    up_down.terms[0] = (arrays[0], up_down.terms[0][1])
    branch_came = swap_mp(branch_b)
    steps = len(up_down.orders)
    step = up_down.scatter(1)
    away, kept = tail_gradient(
        core_list, grads, normed1, own_context, grad_branch, other_context, branch_other, behind=(step,)
    )
    (first_a, first_b, stack_sums), (kept,) = by_inputs(grads, far(w_stack), behind=(away,), through=(kept,))
    tail = Sum(kept, swap_dp(away, 1, count), place, count)
    came = swap_mp(first_b)
    tail.scatter(0)
    for k in range(2, steps):
        up_down.scatter(k)
        step = tail.scatter(k - 1)
    (grad_tokens, sums_first, output), (kept,) = last(
        first_a, came, tokens, grad_hidden, first_gain, b_down, hidden, branch_a, branch_came,
        behind=(step,), through=(tail.terms[0][0],),
    )
    tail.terms[0] = (kept, tail.terms[0][1])
    tail.scatter(steps - 1)
    up_down.turn()
    small = jnp.concatenate([sums_first[:2], sums[:4]], axis=0)
    small = small + swap_mp(small)
    columns = small.shape[1]
    split = jnp.concatenate([stack_sums[0, :width], stack_sums[0, 2 * width :], grad_bupward[0]])
    small = jnp.concatenate([small, split.reshape(-1, columns)], axis=0)
    small = jnp.pad(small, ((0, -small.shape[0] % 4), (0, 0)))
    up_down.gather(steps - 1)
    tail.turn(sums=small)
    for k in range(steps - 1, 0, -1):
        tail.gather(k)
        up_down.gather(k - 1)
    tail.gather(0)
    grad_wquery, grad_wkey, grad_wvalue, grad_woutput, *small = tail_finish(
        core_list, tail.block, tail.came, tail.sums
    )
    grad_upward, grad_down = up_down_finish(core_list, up_down.block, up_down.came)
    return (
        output,
        grad_tokens,
        small[0],
        small[1],
        grad_wquery,
        small[6],
        grad_wkey,
        grad_wvalue,
        small[7],
        grad_woutput,
        small[2],
        small[3],
        small[4],
        grad_upward,
        small[8],
        grad_down,
        small[5],
    )


def solution(mesh):
    in_specs = (
        P(("dp", "mp"), None),
        P("dp", None),
        P(),
        P(),
        P(None, "mp"),
        P("mp"),
        P(None, "mp"),
        P(None, "mp"),
        P("mp"),
        P("mp", None),
        P(),
        P(),
        P(),
        P(None, "mp"),
        P("mp"),
        P("mp", None),
        P(),
        P(("dp", "mp"), None),
    )
    out_specs = (
        P(("dp", "mp"), None),
        P(("dp", "mp"), None),
        P(),
        P(),
        P(None, "mp"),
        P("mp"),
        P(None, "mp"),
        P(None, "mp"),
        P("mp"),
        P("mp", None),
        P(),
        P(),
        P(),
        P(None, "mp"),
        P("mp"),
        P("mp", None),
        P(),
    )
    return jax.shard_map(
        functools.partial(local, mesh.shape["dp"]), mesh=mesh, in_specs=in_specs, out_specs=out_specs, check_vma=False)
```

```python
import functools

import jax
import jax.numpy as jnp
from jax import lax
from jax.experimental import pallas as pl
from jax.experimental.pallas import tpu as pltpu
from jax.sharding import PartitionSpec as P

HEAD = 64
GROUP = 3
BLOCK = 512
epsilon = 1e-06
masked_score = -1e30
low, wide = jnp.bfloat16, jnp.float32
params = pltpu.CompilerParams(vmem_limit_bytes=24 << 20)


def cost(flops, moved, exps=0):
    return pl.CostEstimate(flops=flops, bytes_accessed=moved, transcendentals=exps)


def whole(array):
    return pl.BlockSpec(array.shape, lambda *_: (0,) * len(array.shape))


def shaped(shape, kind):
    return jax.ShapeDtypeStruct(shape, kind)


def stored(shape, kind):
    return pltpu.HBM(shape, kind)


def ordered_call(
    kernel, args, in_specs, out_specs, out_shape, behind=(), through=(), prefetch=0, grid=(), scratch=(), **rest
):
    count, outputs = len(args), len(out_shape)
    skipped = len(behind) + len(through)
    place, kept = pl.BlockSpec(memory_space=pl.ANY), pl.BlockSpec(memory_space=pltpu.HBM)

    def body(*refs):
        given, refs = refs[:count], refs[count + skipped :]
        kernel(*given, *refs[:outputs], *refs[outputs + len(through) :])

    first = count + len(behind)
    out = pl.pallas_call(
        body,
        grid_spec=pltpu.PrefetchScalarGridSpec(
            num_scalar_prefetch=prefetch,
            grid=grid,
            in_specs=list(in_specs) + [place] * len(behind) + [kept] * len(through),
            out_specs=list(out_specs) + [kept] * len(through),
            scratch_shapes=list(scratch),
        ),
        out_shape=list(out_shape) + [stored(a.shape, a.dtype) for a in through],
        input_output_aliases={first + k: outputs + k for k in range(len(through))},
        compiler_params=params,
        **rest,
    )(*args, *behind, *through)
    return list(out[:outputs]), list(out[outputs:])


def far(array):
    return pltpu.with_memory_space_constraint(array, pltpu.HBM)


def mm(left, right, left_dim, right_dim):
    return lax.dot_general(
        left, right, (((left_dim,), (right_dim,)), ((), ())), preferred_element_type=wide
    )


def normalize(values, gain, shift):
    centred = values - jnp.mean(values, axis=-1, keepdims=True)
    spread = jnp.mean(centred * centred, axis=-1, keepdims=True)
    return centred * lax.rsqrt(spread + epsilon) * gain + shift


def normalize_back(values, gain, grad):
    centred = values - jnp.mean(values, axis=-1, keepdims=True)
    inverse = lax.rsqrt(jnp.mean(centred * centred, axis=-1, keepdims=True) + epsilon)
    unit = centred * inverse
    scaled = grad * gain
    by_values = inverse * (
        scaled
        - jnp.mean(scaled, axis=-1, keepdims=True)
        - unit * jnp.mean(scaled * unit, axis=-1, keepdims=True)
    )
    return by_values, jnp.sum(grad * unit, axis=0), jnp.sum(grad, axis=0)


def split_three(row):
    first = row.astype(low).astype(wide)
    second = (row - first).astype(low).astype(wide)
    return first, second, row - first - second


def head_rows(part, width, head):
    return pl.ds(pl.multiple_of(part * width + head * HEAD, HEAD), HEAD)


def project_kernel(
    side_ref, tokens_ref, gain_ref, shift_ref, query_ref, key_ref, value_ref, b_ref, tissue_ref,
    qkv_ref, normed_ref, w_ref, bias_ref
):
    normed = normalize(tokens_ref[...].astype(wide), gain_ref[...][None], shift_ref[...][None]).astype(low)
    normed_ref[...] = normed
    width = query_ref.shape[1]
    for part, ref in enumerate((query_ref, key_ref, value_ref)):
        at = slice(part * width, (part + 1) * width)
        turned = ref[...].T
        w_ref[at] = turned
        qkv_ref[at] = (mm(turned, normed, 1, 1) + b_ref[at]).astype(low)
    own = tokens_ref.shape[0]
    bias = jnp.where(tissue_ref[...] > 0, 0.0, masked_score)
    turned = jnp.concatenate([bias[:, own:], bias[:, :own]], axis=1)
    bias = jnp.where(side_ref[0] == 0, bias, turned)
    index = lax.broadcasted_iota(jnp.int32, bias_ref.shape, 0)
    bias_ref[...] = jnp.where(index == 0, bias, 0.0).astype(low)


def project(side, tokens, gain, shift, w_query, w_key, w_value, b, tissue):
    rows, features = tokens.shape
    width = w_query.shape[1]
    vmem = pl.BlockSpec(memory_space=pltpu.VMEM)
    return pl.pallas_call(
        project_kernel,
        name="project_own_rows",
        in_specs=[pl.BlockSpec(memory_space=pltpu.SMEM)] + [vmem] * 8,
        out_specs=[vmem] * 4,
        out_shape=[
            shaped((3 * width, rows), low),
            shaped((rows, features), low),
            shaped((3 * width, features), low),
            shaped((16, tissue.shape[1]), low),
        ],
        compiler_params=params,
        cost_estimate=cost(10**9, 5 * 10**6),
    )(side, tokens, gain, shift, w_query, w_key, w_value, b, tissue)


def attention_forward_kernel(
    own_ref, own_normed_ref, other_ref, gain_ref, shift_ref, w_ref, b_ref, bias_ref,
    qkv_ref, own_context_ref, other_context_ref, exact_ref, log_ref, normed_ref
):
    group = pl.program_id(0)
    own = other_ref.shape[0]
    rows = 2 * own
    width = w_ref.shape[0] // 3

    @pl.when(group == 0)
    def _():
        normed = normalize(other_ref[...].astype(wide), gain_ref[...][None], shift_ref[...][None]).astype(low)
        normed_ref[:own] = own_normed_ref[...]
        normed_ref[own:] = normed
        for part in range(3):
            at = slice(part * width, (part + 1) * width)
            qkv_ref[at, :own] = own_ref[at]
            qkv_ref[at, own:] = (mm(w_ref[at], normed, 1, 1) + b_ref[at]).astype(low)

    index = lax.broadcasted_iota(jnp.int32, (16, rows), 0)
    ones = jnp.where(index == 0, 1.0, 0.0).astype(low)
    for local_head in range(GROUP):
        head = group * GROUP + local_head
        queries = qkv_ref[head_rows(0, width, head)] * jnp.array(HEAD**-0.5, low)
        keys = jnp.concatenate([qkv_ref[head_rows(1, width, head)], bias_ref[...]], axis=0).T
        values = qkv_ref[head_rows(2, width, head)]
        scores = mm(keys, jnp.concatenate([queries, ones], axis=0), 1, 0)
        highest = jnp.max(scores, axis=0, keepdims=True)
        powers = jnp.exp(scores - highest)
        total = jnp.sum(powers, axis=0, keepdims=True)
        log_ref[local_head] = highest + jnp.log(total)
        context = mm(values, powers.astype(low), 1, 0) * (1.0 / total)
        at = slice(local_head * HEAD, (local_head + 1) * HEAD)
        exact_ref[at] = context
        context = context.astype(low)
        own_context_ref[at] = context[:, :own]
        other_context_ref[at] = context[:, own:]


def attention_forward(own, own_normed, other, gain, shift, w, b, bias):
    count, features = other.shape
    width = w.shape[0] // 3
    rows = 2 * count
    by_head = lambda columns: pl.BlockSpec((GROUP * HEAD, columns), lambda group: (group, 0))
    args = (own, own_normed, other, gain, shift, w, b, bias)
    return pl.pallas_call(
        attention_forward_kernel,
        name="attention_forward",
        grid=(width // HEAD // GROUP,),
        in_specs=[whole(a) for a in args],
        out_specs=[
            pl.BlockSpec((3 * width, rows), lambda group: (0, 0)),
            by_head(count),
            by_head(count),
            by_head(rows),
            pl.BlockSpec((GROUP, 1, rows), lambda group: (group, 0, 0)),
            pl.BlockSpec((rows, features), lambda group: (0, 0)),
        ],
        out_shape=[
            stored((3 * width, rows), low),
            shaped((width, count), low),
            shaped((width, count), low),
            stored((width, rows), wide),
            shaped((width // HEAD, 1, rows), wide),
            stored((rows, features), low),
        ],
        compiler_params=params,
        cost_estimate=cost(10 * 10**9, 10**7, 4 * 10**6),
    )(*args)


def attention_backward_kernel(qkv_ref, exact_ref, log_ref, bias_ref, own_grad_ref, other_grad_ref, out_ref):
    rows = qkv_ref.shape[1]
    width = qkv_ref.shape[0] // 3
    scale = HEAD**-0.5
    index = lax.broadcasted_iota(jnp.int32, (16, rows), 0)

    def stack(top, *extra):
        block = jnp.zeros((16, rows), wide)
        for place, row in enumerate(extra):
            block = jnp.where(index == place, row, block)
        return jnp.concatenate([top, block.astype(low)], axis=0)

    bias = bias_ref[0:1].astype(wide)
    for local_head in range(GROUP):
        head = pl.program_id(0) * GROUP + local_head
        at = slice(local_head * HEAD, (local_head + 1) * HEAD)
        queries = qkv_ref[head_rows(0, width, head)] * jnp.array(scale, low)
        keys = qkv_ref[head_rows(1, width, head)]
        values = qkv_ref[head_rows(2, width, head)]
        grads = jnp.concatenate([own_grad_ref[at], other_grad_ref[at]], axis=1)
        overlap = jnp.sum(grads.astype(wide) * exact_ref[at], axis=0, keepdims=True)
        queries_more = stack(queries, 1.0, *split_three(-log_ref[local_head]))
        keys_more = stack(keys, bias, 1.0, 1.0, 1.0).T
        grads_more = stack(grads, *split_three(-overlap))
        values_more = stack(values, 1.0, 1.0, 1.0).T
        chances = jnp.exp(mm(keys_more, queries_more, 1, 0))
        out_ref[head_rows(2, width, head)] = mm(grads, chances.astype(low), 1, 1).astype(low)
        grad_scores = (chances * mm(values_more, grads_more, 1, 0)).astype(low)
        out_ref[head_rows(0, width, head)] = (mm(keys, grad_scores, 1, 0) * scale).astype(low)
        out_ref[head_rows(1, width, head)] = mm(queries, grad_scores, 1, 1).astype(low)


def attention_backward(qkv, exact, logs, bias, own_grad, other_grad, behind, through):
    rows = qkv.shape[1]
    width = qkv.shape[0] // 3
    by_head = lambda columns: pl.BlockSpec((GROUP * HEAD, columns), lambda group: (group, 0))
    return ordered_call(
        attention_backward_kernel,
        (qkv, exact, logs, bias, own_grad, other_grad),
        [
            whole(qkv),
            by_head(rows),
            pl.BlockSpec((GROUP, 1, rows), lambda group: (group, 0, 0)),
            whole(bias),
            by_head(rows // 2),
            by_head(rows // 2),
        ],
        [whole(qkv)],
        [shaped(qkv.shape, low)],
        behind=behind,
        through=through,
        grid=(width // HEAD // GROUP,),
        name="attention_backward",
        cost_estimate=cost(10 * 10**9, 10**7, 4 * 10**6),
    )


def gelu_both(values):
    below = 0.5 * (1.0 + lax.erf(values * (0.5**0.5)))
    density = jnp.exp(values * values * -0.5) * (2.0 * jnp.pi) ** -0.5
    return values * below, below + values * density


def feed_forward_kernel(
    tokens_ref, mine_ref, peer_ref, w_mine_ref, w_peer_ref, b_ref, gain_ref, shift_ref, cotangent_ref,
    up_ref, b_up_ref, down_ref, *refs, other
):
    if other:
        core_ref, *more = refs[:6]
        hidden_ref, grad_normed_ref, branch_ref, grad_b_ref, away_ref, kept_ref, *scratch = refs[6:]
        normed_ref, grad_sum, sum_ = scratch
    else:
        normed_ref, activated_ref, grad_pre_ref, grad_normed_ref, branch_ref, grad_b_ref, grad_sum, sum_ = refs
    step = pl.program_id(0)

    @pl.when(step == 0)
    def _():
        attention = mm(mine_ref[...], w_mine_ref[...], 0, 0) + mm(peer_ref[...], w_peer_ref[...], 0, 0)
        hidden = tokens_ref[...].astype(wide) + (attention + b_ref[...][None])
        normed = normalize(hidden, gain_ref[...][None], shift_ref[...][None]).astype(low)
        normed_ref[...] = normed
        grad_sum[...] = jnp.zeros_like(grad_sum)
        sum_[...] = jnp.zeros_like(sum_)
        if other:
            hidden_ref[...] = hidden

    up, down = up_ref[...], down_ref[...]
    pre_gelu = mm(normed_ref[...], up, 1, 0) + b_up_ref[...]
    grad_active = mm(cotangent_ref[...], down, 1, 1)
    activated, slope = gelu_both(pre_gelu)
    activated = activated.astype(low)
    grad_pre = (grad_active * slope).astype(low)
    sums = jnp.sum(grad_pre.astype(wide), axis=0, keepdims=True)
    grad_sum[...] += mm(grad_pre, up, 1, 1)
    sum_[...] += mm(activated, down, 1, 0)
    if other:
        other_normed_ref, other_cotangent_ref, other_activated_ref, other_grad_pre_ref, other_grad_b_ref = more
        grad_b_ref[...] = sums + other_grad_b_ref[...]
        grad_down = mm(activated, cotangent_ref[...], 0, 0)
        grad_down = (grad_down + mm(other_activated_ref[...], other_cotangent_ref[...], 0, 0)).astype(low)
        grad_up = mm(grad_pre, normed_ref[...], 0, 0)
        grad_up = (grad_up + mm(other_grad_pre_ref[...], other_normed_ref[...], 0, 0)).astype(low)
        is_first = core_ref[0] == 0
        away_ref[...] = jnp.where(is_first, grad_up, grad_down)
        kept_ref[...] = jnp.where(is_first, grad_down, grad_up)
    else:
        grad_b_ref[...] = sums
        activated_ref[...] = activated
        grad_pre_ref[...] = grad_pre

    @pl.when(step == pl.num_programs(0) - 1)
    def _():
        grad_normed_ref[...] = grad_sum[...].astype(low)
        branch_ref[...] = sum_[...].astype(low)


def feed_forward(tokens, mine, peer, w_mine, w_peer, b, gain, shift, cotangent, up, b_up, down, other=()):
    rows, features = tokens.shape
    units = up.shape[1]
    block = BLOCK
    by_rows = pl.BlockSpec((rows, block), lambda step: (0, step))
    by_unit = pl.BlockSpec((1, block), lambda step: (0, step))
    by_up = pl.BlockSpec((features, block), lambda step: (0, step))
    by_down = pl.BlockSpec((block, features), lambda step: (step, 0))
    plain = shaped((rows, features), low)
    scratch = [pltpu.VMEM((rows, features), wide), pltpu.VMEM((rows, features), wide)]
    if other:
        out_specs = [whole(tokens)] * 3 + [by_unit, by_down, by_down]
        out_shape = [stored((rows, features), wide), plain, stored((rows, features), low), shaped((1, units), wide)]
        out_shape += [stored((units, features), low)] * 2
        scratch = [pltpu.VMEM((rows, features), low)] + scratch
    else:
        out_specs = [whole(tokens), by_rows, by_rows, whole(tokens), whole(tokens), by_unit]
        out_shape = [plain, shaped((rows, units), low), shaped((rows, units), low), plain]
        out_shape += [stored((rows, features), low)]
        out_shape += [shaped((1, units), wide)]
    return pl.pallas_call(
        functools.partial(feed_forward_kernel, other=bool(other)),
        name="feed_forward",
        grid=(units // block,),
        in_specs=[whole(a) for a in (tokens, mine, peer, w_mine, w_peer, b, gain, shift, cotangent)]
        + [by_up, by_unit, by_down]
        + (
            [pl.BlockSpec(memory_space=pltpu.SMEM), whole(other[1]), whole(other[2]), by_rows, by_rows, by_unit]
            if other
            else []
        ),
        out_specs=out_specs,
        out_shape=out_shape,
        scratch_shapes=scratch,
        compiler_params=params,
        cost_estimate=cost(5 * 10**9, 10**7, 10**6),
    )(tokens, mine, peer, w_mine, w_peer, b, gain, shift, cotangent, up, b_up, down, *other)


def middle_kernel(
    part_ref, came_ref, hidden_ref, cotangent_ref, gain_ref, w_mine_ref, w_peer_ref,
    grad_hidden_ref, branch_ref, mine_ref, peer_ref, sums_ref
):
    grad = part_ref[...].astype(wide) + came_ref[...].astype(wide)
    cotangent = cotangent_ref[...].astype(wide)
    by_hidden, by_gain, by_shift = normalize_back(hidden_ref[...], gain_ref[...][None], grad)
    grad_hidden = by_hidden + cotangent
    grad_hidden_ref[...] = grad_hidden
    branch = grad_hidden.astype(low)
    branch_ref[...] = branch
    mine_ref[...] = mm(w_mine_ref[...], branch, 1, 1).astype(low)
    peer_ref[...] = mm(w_peer_ref[...], branch, 1, 1).astype(low)
    sums_ref[...] = jnp.zeros_like(sums_ref)
    sums_ref[0:1] = jnp.sum(branch.astype(wide), axis=0, keepdims=True)
    sums_ref[1:2] = by_gain[None]
    sums_ref[2:3] = by_shift[None]
    sums_ref[3:4] = jnp.sum(cotangent, axis=0, keepdims=True)


def middle(part, came, hidden, cotangent, gain, w_mine, w_peer, through):
    rows, features = part.shape
    width = w_mine.shape[0]
    vmem = pl.BlockSpec(memory_space=pltpu.VMEM)
    return ordered_call(
        middle_kernel,
        (part, came, hidden, cotangent, gain, w_mine, w_peer),
        [vmem] * 7,
        [vmem] * 5,
        [
            stored((rows, features), wide),
            stored((rows, features), low),
            stored((width, rows), low),
            stored((width, rows), low),
            shaped((8, features), wide),
        ],
        through=through,
        name="second_norm_backward",
        cost_estimate=cost(10**9, 5 * 10**6),
    )


def last_kernel(
    part_ref, came_ref, tokens_ref, grad_hidden_ref, gain_ref, b_ref, hidden_ref, branch_ref, branch_came_ref,
    out_ref, sums_ref, output_ref
):
    grad = part_ref[...].astype(wide) + came_ref[...].astype(wide)
    by_tokens, by_gain, by_shift = normalize_back(tokens_ref[...].astype(wide), gain_ref[...][None], grad)
    out_ref[...] = grad_hidden_ref[...] + by_tokens
    sums_ref[...] = jnp.zeros_like(sums_ref)
    sums_ref[0:1] = by_gain[None]
    sums_ref[1:2] = by_shift[None]
    branch = branch_ref[...].astype(wide) + branch_came_ref[...].astype(wide)
    output_ref[...] = (hidden_ref[...] + (branch + b_ref[...][None])).astype(low)


def last(part, came, tokens, grad_hidden, gain, b, hidden, branch, branch_came, behind, through):
    rows, features = part.shape
    vmem = pl.BlockSpec(memory_space=pltpu.VMEM)
    return ordered_call(
        last_kernel,
        (part, came, tokens, grad_hidden, gain, b, hidden, branch, branch_came),
        [vmem] * 9,
        [vmem] * 3,
        [shaped((rows, features), wide), shaped((8, features), wide), shaped((rows, features), low)],
        behind=behind,
        through=through,
        name="first_norm_backward",
        cost_estimate=cost(10**8, 5 * 10**6),
    )


def by_inputs_kernel(grads_ref, w_ref, own_ref, other_ref, sums_ref):
    own = own_ref.shape[0]
    grads = grads_ref[...]
    other_ref[...] = mm(grads[:, own:], w_ref[...], 0, 0).astype(low)
    own_ref[...] = mm(grads[:, :own], w_ref[...], 0, 0).astype(low)
    sums_ref[...] = mm(jnp.ones((8, grads.shape[1]), low), grads, 1, 1)


def by_inputs(grads, w, behind, through):
    rows, features = grads.shape[1] // 2, w.shape[1]
    vmem = pl.BlockSpec(memory_space=pltpu.VMEM)
    return ordered_call(
        by_inputs_kernel,
        (grads, w),
        [vmem] * 2,
        [vmem] * 3,
        [
            stored((rows, features), low),
            stored((rows, features), low),
            shaped((8, grads.shape[0]), wide),
        ],
        behind=behind,
        through=through,
        name="first_normed_gradient",
        cost_estimate=cost(2 * 10**9, 5 * 10**6),
    )


def tail_gradient_kernel(
    core_ref, grads_ref, normed_ref, own_context_ref, own_branch_ref, other_context_ref, other_branch_ref,
    away_ref, kept_ref
):
    step = pl.program_id(0)
    block = tail_block(step, core_ref[0])

    def put(total):
        @pl.when(step < 2)
        def _():
            away_ref[...] = total.astype(low)

        @pl.when(step >= 2)
        def _():
            kept_ref[...] = total

    @pl.when(block < 3)
    def _():
        put(mm(grads_ref[...], normed_ref[...], 1, 0))

    @pl.when(block == 3)
    def _():
        put(
            mm(own_context_ref[...], own_branch_ref[...], 1, 0)
            + mm(other_context_ref[...], other_branch_ref[...], 1, 0)
        )


def tail_block(step, core):
    side = jnp.where(step < 2, 1 - core, core)
    return side * 2 + (step & 1)


def tail_gradient(core, grads, normed, own_context, own_branch, other_context, other_branch, behind):
    width, features = own_context.shape[0], normed.shape[1]
    rest = (normed, own_context, own_branch, other_context, other_branch)
    return ordered_call(
        tail_gradient_kernel,
        (core, grads, *rest),
        [
            pl.BlockSpec(
                (width, grads.shape[1]),
                lambda step, core_ref: (jnp.minimum(tail_block(step, core_ref[0]), 2), 0),
            )
        ]
        + [whole(a) for a in rest],
        [
            pl.BlockSpec((width, features), lambda step, _: (jnp.minimum(step, 1), 0)),
            pl.BlockSpec((width, features), lambda step, _: (jnp.maximum(step - 2, 0), 0)),
        ],
        [stored((2 * width, features), low), stored((2 * width, features), wide)],
        behind=behind,
        prefetch=1,
        grid=(4,),
        name="tail_gradient",
        cost_estimate=cost(2 * 10**9, 10**7),
    )[0]


def after(value, *others):
    return lax.optimization_barrier((value, *others))[0]


def swap_mp(value):
    return lax.ppermute(value, "mp", [(0, 1), (1, 0)])


def swap_dp(value, mask, count):
    return lax.ppermute(value, "dp", [(i, i ^ mask) for i in range(count)])


def rows_at(value, at, rows):
    return lax.dynamic_slice_in_dim(value, at * rows, rows, 0)


def rows_set(value, block, at):
    return lax.dynamic_update_slice_in_dim(value, block, at * block.shape[0], 0)


class Sum:
    def __init__(self, kept, came, place, count):
        self.count, self.rows = count, kept.shape[0]
        self.terms, self.came = [(kept, 0)], came
        self.core, chip = place & 1, place >> 1
        bits = (count // 2).bit_length() - 1
        other = [1, 0] if bits > 1 else [0]
        self.orders = list(zip(range(bits), other + list(range(2, bits))))
        self.bits = [(chip >> jnp.where(self.core == 0, a, b)) & 1 for a, b in self.orders]
        self.sums = None

    def swap(self, value, step):
        partner = lambda i: i ^ (2 << self.orders[step][i & 1])
        return lax.ppermute(value, "dp", [(i, partner(i)) for i in range(self.count)])

    def rows_of(self, shift, rows):
        total = 0.0
        for array, start in self.terms:
            total = total + lax.dynamic_slice_in_dim(array, start + shift, rows, 0).astype(wide)
        return total.astype(low)

    def scatter(self, step):
        self.terms.append((self.came, 0))
        self.rows //= 2
        sent = self.rows_of((1 - self.bits[step]) * self.rows, self.rows)
        self.came = self.swap(sent, step)
        self.terms = [(array, start + self.bits[step] * self.rows) for array, start in self.terms]
        return sent

    def turn(self, sums=None):
        self.terms.append((self.came, 0))
        self.block = self.rows_of(0, self.rows)
        self.sums = sums
        return self.send(len(self.orders) - 1)

    def send(self, step):
        sent = self.block if self.sums is None else jnp.concatenate([pack_rows(self.sums), self.block], axis=0)
        self.came = self.swap(sent, step) if step >= 0 else swap_dp(sent, 1, self.count)
        return sent

    def gather(self, step):
        came = self.came
        extra = came.shape[0] - self.block.shape[0]
        if extra:
            self.sums = self.sums + widen(came[:extra])
        mine, other = self.block, came[extra:]
        self.block = jnp.where(
            self.bits[step] == 0,
            jnp.concatenate([mine, other], axis=0),
            jnp.concatenate([other, mine], axis=0),
        )
        return self.send(step - 1)


def widen(pair):
    rows = pair.shape[0] // 2
    return pair[:rows].astype(wide) + pair[rows:].astype(wide)


def pack_rows(rows):
    top = lax.reduce_precision(rows, exponent_bits=8, mantissa_bits=7)
    return jnp.concatenate([top, rows - top], axis=0).astype(low)


def up_down_finish_kernel(core_ref, mine_ref, other_ref, up_ref, down_ref):
    for core in range(2):

        @pl.when(core_ref[0] == core)
        def _():
            down, up = (mine_ref, other_ref) if core == 0 else (other_ref, mine_ref)
            down_ref[...] = down[...].astype(wide)
            up_ref[...] = up[...].astype(wide).T


def up_down_finish(core, mine, other):
    units, features = mine.shape
    block = 256
    by_unit = pl.BlockSpec((block, features), lambda step: (step, 0))
    return pl.pallas_call(
        up_down_finish_kernel,
        name="up_down_finish",
        grid=(units // block,),
        in_specs=[pl.BlockSpec(memory_space=pltpu.SMEM), by_unit, by_unit],
        out_specs=[pl.BlockSpec((features, block), lambda step: (0, step)), by_unit],
        out_shape=[shaped((features, units), wide), shaped((units, features), wide)],
        compiler_params=params,
        cost_estimate=cost(10**6, 10**7),
    )(core, mine, other)


def tail_finish_kernel(core_ref, half_ref, came_ref, small_ref, *refs):
    extra = came_ref.shape[0] - half_ref.shape[0]
    rows = extra // 2
    small = small_ref[...] + (came_ref[:rows].astype(wide) + came_ref[rows:extra].astype(wide))
    columns = small.shape[1]
    for row in range(6):
        refs[4 + row][...] = small[row]
    refs[10][...] = small[6, : columns // 2]
    refs[11][...] = small[6, columns // 2 :]
    refs[12][:columns] = small[7]
    refs[12][columns:] = small[8]
    for core in range(2):

        @pl.when(core_ref[0] == core)
        def _():
            width = half_ref.shape[0] // 2
            mine, other = (half_ref, 0), (came_ref, extra)
            (first, at), (second, to) = (mine, other) if core == 0 else (other, mine)
            refs[0][...] = first[at : at + width].astype(wide).T
            refs[1][...] = first[at + width : at + 2 * width].astype(wide).T
            refs[2][...] = second[to : to + width].astype(wide).T
            refs[3][...] = second[to + width : to + 2 * width].astype(wide)


def tail_finish(core, half, came, small):
    rows, features = half.shape
    width = rows // 2
    vmem = pl.BlockSpec(memory_space=pltpu.VMEM)
    vectors = [features] * 6 + [features // 2] * 2 + [2 * features]
    return pl.pallas_call(
        tail_finish_kernel,
        name="tail_finish",
        in_specs=[pl.BlockSpec(memory_space=pltpu.SMEM), vmem, vmem, vmem],
        out_specs=[vmem] * 13,
        out_shape=[shaped((features, width), wide)] * 3
        + [shaped((width, features), wide)]
        + [shaped((n,), wide) for n in vectors],
        compiler_params=params,
        cost_estimate=cost(10**6, 10**7),
    )(core, half, came, small)


def local(
    count,
    tokens,
    tissue,
    first_gain,
    first_shift,
    w_query,
    b_query,
    w_key,
    w_value,
    b_value,
    w_output,
    b_output,
    second_gain,
    second_shift,
    w_upward,
    b_upward,
    w_down,
    b_down,
    cotangent,
):
    place, side = lax.axis_index("dp"), lax.axis_index("mp")
    core = place & 1
    core_list = core.reshape(1)
    own = tokens.shape[0]
    width = w_query.shape[1]
    tokens_other = swap_mp(tokens)
    half_width = width // 2
    w_half = swap_mp(after(rows_at(w_output, core, half_width), tokens_other))
    cotangent_other = swap_mp(after(cotangent, tokens_other))
    b_stack = jnp.concatenate([b_query, jnp.zeros_like(b_query), b_value])[:, None]
    own_qkv, own_normed, w_stack, bias = project(
        side.reshape(1), tokens, first_gain, first_shift, w_query, w_key, w_value, b_stack, tissue
    )

    qkv, own_context, other_context, exact, logs, normed1 = attention_forward(
        own_qkv, own_normed, after(tokens_other, own_qkv), first_gain, first_shift, w_stack, b_stack, bias
    )
    w_traded = swap_dp(after(w_half, own_context), 1, count)
    w_peer = jnp.where(
        core == 0,
        jnp.concatenate([w_half, w_traded], axis=0),
        jnp.concatenate([w_traded, w_half], axis=0),
    )
    peer_other = swap_mp(own_context)
    peer_own = swap_mp(after(other_context, peer_other))
    b_up = b_upward[None]
    shared = (far(w_upward), b_up, far(w_down))
    second = (b_output, second_gain, second_shift)
    normed_b, active_b, pre_b, part_b, branch_b, sum_b = feed_forward(
        tokens_other, other_context, peer_other, w_output, w_peer, *second, cotangent_other, *shared
    )
    came = swap_mp(part_b)
    hidden, part_a, branch_a, grad_bupward, up_down_away, up_down_kept = feed_forward(
        after(tokens, part_b), own_context, peer_own, w_output, w_peer, *second, cotangent, *shared,
        other=(core_list, normed_b, cotangent_other, active_b, pre_b, sum_b),
    )
    (grad_hidden, grad_branch, mine_own, peer_grad, sums), (up_down_away,) = middle(
        part_a, came, hidden, cotangent, second_gain, w_output, w_peer, through=(up_down_away,)
    )
    up_down = Sum(up_down_kept, swap_dp(up_down_away, 1, count), place, count)
    mine_other = swap_mp(peer_grad)
    branch_other = swap_mp(after(grad_branch, mine_other))
    step = up_down.scatter(0)
    (grads,), (branch_b, *arrays) = attention_backward(
        far(qkv), far(exact), logs, bias, mine_own, mine_other, behind=(step,), through=(branch_b, up_down.terms[0][0])
    )
    up_down.terms[0] = (arrays[0], up_down.terms[0][1])
    branch_came = swap_mp(branch_b)
    steps = len(up_down.orders)
    step = up_down.scatter(1)
    away, kept = tail_gradient(
        core_list, grads, normed1, own_context, grad_branch, other_context, branch_other, behind=(step,)
    )
    (first_a, first_b, stack_sums), (kept,) = by_inputs(grads, far(w_stack), behind=(far(away),), through=(kept,))
    tail = Sum(kept, swap_dp(away, 1, count), place, count)
    came = swap_mp(first_b)
    tail.scatter(0)
    for k in range(2, steps):
        up_down.scatter(k)
        step = tail.scatter(k - 1)
    (grad_tokens, sums_first, output), (kept,) = last(
        far(first_a), came, far(tokens), far(grad_hidden), first_gain, b_down, far(hidden), far(branch_a), branch_came,
        behind=(step,), through=(tail.terms[0][0],),
    )
    tail.terms[0] = (kept, tail.terms[0][1])
    tail.scatter(steps - 1)
    up_down.turn()
    small = jnp.concatenate([sums_first[:2], sums[:4]], axis=0)
    small = small + swap_mp(small)
    columns = small.shape[1]
    split = jnp.concatenate([stack_sums[0, :width], stack_sums[0, 2 * width :], grad_bupward[0]])
    small = jnp.concatenate([small, split.reshape(-1, columns)], axis=0)
    small = jnp.pad(small, ((0, -small.shape[0] % 4), (0, 0)))
    up_down.gather(steps - 1)
    tail.turn(sums=small)
    for k in range(steps - 1, 0, -1):
        tail.gather(k)
        up_down.gather(k - 1)
    tail.gather(0)
    grad_wquery, grad_wkey, grad_wvalue, grad_woutput, *small = tail_finish(
        core_list, tail.block, tail.came, tail.sums
    )
    grad_upward, grad_down = up_down_finish(core_list, up_down.block, up_down.came)
    return (
        output,
        grad_tokens,
        small[0],
        small[1],
        grad_wquery,
        small[6],
        grad_wkey,
        grad_wvalue,
        small[7],
        grad_woutput,
        small[2],
        small[3],
        small[4],
        grad_upward,
        small[8],
        grad_down,
        small[5],
    )


def solution(mesh):
    in_specs = (
        P(("dp", "mp"), None),
        P("dp", None),
        P(),
        P(),
        P(None, "mp"),
        P("mp"),
        P(None, "mp"),
        P(None, "mp"),
        P("mp"),
        P("mp", None),
        P(),
        P(),
        P(),
        P(None, "mp"),
        P("mp"),
        P("mp", None),
        P(),
        P(("dp", "mp"), None),
    )
    out_specs = (
        P(("dp", "mp"), None),
        P(("dp", "mp"), None),
        P(),
        P(),
        P(None, "mp"),
        P("mp"),
        P(None, "mp"),
        P(None, "mp"),
        P("mp"),
        P("mp", None),
        P(),
        P(),
        P(),
        P(None, "mp"),
        P("mp"),
        P("mp", None),
        P(),
    )
    return jax.shard_map(
        functools.partial(local, mesh.shape["dp"]), mesh=mesh, in_specs=in_specs, out_specs=out_specs, check_vma=False)
```
